32 devices in a mesh: groups: 2 (over y), ctx: 4 (over z), dp: 2 (over x), hp: 2 (over core).
Axes of the slice: x: 2, y: 2, z: 4, core: 2. Of those that a mesh axis runs over, the one named last changes fastest.
Arguments:
- residual: bfloat16 [8, 7168], P(('groups', 'dp'), 'ctx'), parts along dimension 0
- expert_out: bfloat16 [4, 2, 16, 7168], P(('groups', 'dp'), None, None, 'ctx'), parts along dimension 0, may hold values from -6 to 6
- combine_slot: int32 [8, 8], P(('groups', 'dp')), parts along dimension 0, may hold values from 0 to 31, as said below
- combine_gate: float32 [8, 8], P(('groups', 'dp')), parts along dimension 0, may hold values from 0.05 to 0.6
- attn_gain: float32 [7168], P('ctx'), may hold values from 0.1 to 1.9
- query_down: bfloat16 [7168, 1536], P('ctx'), may hold values from -0.0625 to 0.0625
- index_gate: bfloat16 [7168, 64], P('ctx'), may hold values from -0.0625 to 0.0625
- latent_gain: float32 [1536], replicated, may hold values from 0.1 to 1.9
- query_up: bfloat16 [1536, 128, 192], P(None, ('ctx', 'hp')), may hold values from -0.15625 to 0.15625
- key_absorb: bfloat16 [128, 128, 512], P(('ctx', 'hp')), may hold values from -0.5 to 0.5
- index_query: bfloat16 [1536, 64, 128], P(None, ('ctx', 'hp')), may hold values from -0.15625 to 0.15625
- value_up: bfloat16 [128, 512, 128], P(('ctx', 'hp')), may hold values from -0.25 to 0.25
- latent_cache: bfloat16 [8, 2048, 576], P(('groups', 'dp'), 'ctx'), parts along dimension 0
- index_keys: bfloat16 [8, 2048, 128], P(('groups', 'dp'), ('ctx', 'hp')), parts along dimension 0, may hold values from -6 to 6
- lengths: int32 [8], P(('groups', 'dp')), parts along dimension 0, may hold values from 512 to 2048, as said below
- block_list: int32 [8, 4], P(('groups', 'dp')), parts along dimension 0, may hold values from 0 to 31, as said below
Outputs:
- hidden: bfloat16 [8, 7168], P(('groups', 'dp'), 'ctx'), parts along dimension 0
- index_scores: float32 [8, 2048], P(('groups', 'dp'), ('ctx', 'hp')), parts along dimension 0
- attn_out: bfloat16 [8, 128, 128], P(('groups', 'dp'), ('ctx', 'hp')), parts along dimension 0
The draws below stay inside these ranges and needn't reach their ends.
There are 2 independent parts, one for each index of `groups`. The reference program is written for one: setup_inputs(seed, part) draws one part's arguments, and reference() takes and returns one part's arrays. A program takes and returns all parts, laid end to end along the dimension named above; an argument that names none is the same for every part. Nothing has to cross between parts.
Inputs may be any that keep to these rules, and one draw needn't show every extreme that they name: `combine_slot`: within one group of 2 rows the slots are distinct; at most 16 of them fall in the range of one source s (s * 16 to s * 16 + 15), and in every group some source has exactly 16. `lengths`: each group of 2 rows holds a row of length exactly 2048. `block_list`: A row's entries are distinct blocks that hold some position below its length, and include block 0 and the block of position lengths - 1.
All inputs are finite; a program needn't handle non-finite values.
Results may differ from the reference program's by a relative error of at most 0.02.
Values may be sent and summed in bfloat16 or wider, within the bound.
No kernel may reach another device: no remote copies, remote signals or barrier semaphores. Data moves between devices by JAX's collectives and lax.ppermute only.
A program may use at most 64 MiB of HBM per device.

```python
import math
import jax
import jax.numpy as jnp
from jax import lax

D = 7168
QLORA = 1536
KVLORA = 512
ROPE = 64
NOPE = 128
VDIM = 128
HEADS = 128
IHEADS = 64
IDIM = 128
TOPE = 8
BLK = 64
RDP = 2
CTX_DEV = 512
ROWS = 4
CTX = 2048
NSEL = 4
CAP = 16
N_CTX = 4
N_DP = 2


def draw_residual(key, part):
    ramp = jnp.arange(D, dtype=jnp.float32) / D
    values = jax.random.normal(key, (ROWS, D), jnp.float32) * (1.0 + 1.2 * ramp)
    return values.astype(jnp.bfloat16)


def draw_latent_cache(key, part):
    base_key = jax.random.fold_in(jax.random.fold_in(key, 3), 0)
    width = KVLORA + ROPE
    base = jax.random.normal(base_key, (ROWS, CTX, width), jnp.float32)
    return base.astype(jnp.bfloat16)


def draw_combine_slot(key, part):

    def group_slots(group_key, group_number):
        full_key, pick_key, shuffle_key = jax.random.split(group_key, 3)
        drawn = jax.random.randint(full_key, (), 0, N_DP).astype(jnp.int32)
        full = jnp.where(group_number == 0, N_DP - 1, drawn).astype(jnp.int32)
        others = jax.random.permutation(pick_key, (N_DP - 1) * CAP)[:RDP * TOPE - CAP].astype(jnp.int32)
        bucket = others // CAP
        others = others + CAP * (bucket >= full).astype(jnp.int32)
        slots = jnp.concatenate([full * CAP + jnp.arange(CAP, dtype=jnp.int32), others])
        slots = jax.random.permutation(shuffle_key, slots)
        return slots.reshape(RDP, TOPE)
    group_keys = jax.random.split(jax.random.fold_in(key, 5), N_DP)
    numbers = jnp.arange(N_DP, dtype=jnp.int32)
    return jax.vmap(group_slots)(group_keys, numbers).reshape(ROWS, TOPE).astype(jnp.int32)


def row_lengths(key):
    first_key, second_key = jax.random.split(jax.random.fold_in(key, 11))
    spans = jax.random.randint(first_key, (N_DP, RDP), CTX // 4, CTX + 1)
    full_row = jax.random.randint(second_key, (N_DP, 1), 0, RDP)
    spans = jnp.where(jnp.arange(RDP, dtype=jnp.int32)[None, :] == full_row, CTX, spans)
    return spans.reshape(ROWS).astype(jnp.int32)


def draw_lengths(key, part):
    return row_lengths(key)


def draw_block_list(key, part):
    spans = row_lengths(key)
    count = CTX // BLK
    live_blocks = (spans + BLK - 1) // BLK
    priority = jax.random.randint(jax.random.fold_in(key, 13), (ROWS, count), 0, 1 << 16)
    block_ids = jnp.arange(count, dtype=jnp.int32)[None, :]
    priority = jnp.where(block_ids >= live_blocks[:, None], -1, priority)
    priority = jnp.where((block_ids == 0) | (block_ids == live_blocks[:, None] - 1), 1 << 17, priority)
    keyed = priority * count + block_ids
    return lax.top_k(keyed, NSEL)[1].astype(jnp.int32)


def block_levels(stream_key, dims, shards, least, high):
    gain = 1.0
    for axis_at, blocks in shards:
        draws = jax.random.uniform(jax.random.fold_in(jax.random.fold_in(stream_key, 6), axis_at), (blocks,), jnp.float32, least / len(shards), high / len(shards))
        gain = gain * jnp.repeat(jnp.exp(draws), dims[axis_at] // blocks).reshape((-1,) + (1,) * (len(dims) - 1 - axis_at))
    return gain


def normal_values(key, dims, scale, limit, cuts=(), kind=jnp.bfloat16):
    values = jax.random.normal(key, dims, jnp.float32) * scale
    if len(cuts) > 0:
        values = block_levels(key, dims, cuts, -0.22, 0.18) * values
    return jnp.clip(values, min=-limit, max=limit).astype(kind)


def setup_inputs(seed: int = 0, part: int = 0) -> dict:
    seeds = jax.random.split(jax.random.key(seed), 17)
    part_keys = jax.random.split(jax.random.fold_in(seeds[16], part), 17)
    residual = draw_residual(jax.random.fold_in(jax.random.fold_in(seeds[16], part), 71), part)
    expert_out = normal_values(part_keys[1], (N_DP, N_DP, CAP, D), 1.0, 6.0, ((0, 2), (3, 4)))
    combine_slot = draw_combine_slot(jax.random.fold_in(jax.random.fold_in(seeds[16], part), 71), part)
    combine_gate = jnp.clip(jnp.exp(math.log(0.6) - 2.4849067 * jax.random.uniform(part_keys[3], (ROWS, TOPE), jnp.float32) ** block_levels(part_keys[3], (ROWS, TOPE), ((0, 2),), -0.2, 0.2)), 0.05, 0.6)
    attn_gain = jnp.clip(1.0 + 0.18 * jax.random.normal(seeds[4], (D,), jnp.float32), 0.1, 1.9)
    query_down = normal_values(seeds[5], (D, QLORA), D ** -0.5, 0.0625, ((0, 4),))
    index_gate = normal_values(seeds[6], (D, IHEADS), D ** -0.5, 0.0625, ((0, 4),))
    latent_gain = jnp.clip(1.0 + 0.18 * jax.random.normal(seeds[7], (QLORA,), jnp.float32), 0.1, 1.9)
    query_up = normal_values(seeds[8], (QLORA, HEADS, NOPE + ROPE), QLORA ** -0.5, 0.15625, ((1, 8),))
    key_absorb = normal_values(seeds[9], (HEADS, NOPE, KVLORA), NOPE ** -0.5, 0.5, ((0, 8),))
    index_query = normal_values(seeds[10], (QLORA, IHEADS, IDIM), QLORA ** -0.5, 0.15625, ((1, 8),))
    value_up = normal_values(seeds[11], (HEADS, KVLORA, VDIM), KVLORA ** -0.5, 0.25, ((0, 8),))
    latent_cache = draw_latent_cache(jax.random.fold_in(jax.random.fold_in(seeds[16], part), 71), part)
    index_keys = normal_values(part_keys[13], (ROWS, CTX, IDIM), 1.0, 6.0, ((0, 2), (1, 8)))
    lengths = draw_lengths(jax.random.fold_in(jax.random.fold_in(seeds[16], part), 71), part)
    block_list = draw_block_list(jax.random.fold_in(jax.random.fold_in(seeds[16], part), 71), part)
    return {"residual": residual, "expert_out": expert_out, "combine_slot": combine_slot, "combine_gate": combine_gate, "attn_gain": attn_gain, "query_down": query_down, "index_gate": index_gate, "latent_gain": latent_gain, "query_up": query_up, "key_absorb": key_absorb, "index_query": index_query, "value_up": value_up, "latent_cache": latent_cache, "index_keys": index_keys, "lengths": lengths, "block_list": block_list}


epsilon = 1e-06
very_low = -1e+30

def rms_scale(values):
    return lax.rsqrt(lax.optimization_barrier(jnp.mean(values * values, axis=-1, keepdims=True)) + epsilon)

def reference(residual, expert_out, combine_slot, combine_gate, attn_gain, query_down, index_gate, latent_gain, query_up, key_absorb, index_query, value_up, latent_cache, index_keys, lengths, block_list):
    buffers = jnp.transpose(expert_out, (1, 0, 2, 3)).reshape(N_DP, N_DP * CAP, D)
    owner = jnp.arange(ROWS, dtype=jnp.int32) // RDP
    picked = buffers[owner[:, None], combine_slot].astype(jnp.float32)
    routed = lax.optimization_barrier(jnp.sum(combine_gate[:, :, None] * picked, axis=1))
    hidden = (residual.astype(jnp.float32) + routed).astype(jnp.bfloat16)
    widened = hidden.astype(jnp.float32)
    normed = (widened * rms_scale(widened) * attn_gain).astype(jnp.bfloat16)
    latent_sum = jnp.dot(normed, query_down, preferred_element_type=jnp.float32)
    gate_sum = jnp.dot(normed, index_gate, preferred_element_type=jnp.float32)
    latent = (latent_sum * rms_scale(latent_sum) * latent_gain).astype(jnp.bfloat16)
    head_gate = gate_sum * IHEADS ** (-0.5)
    projected = jnp.einsum('rq,qnd->rnd', latent.astype(jnp.float32), query_up.astype(jnp.float32)).astype(jnp.bfloat16)
    absorbed = jnp.einsum('rnk,nkc->rnc', projected[:, :, :NOPE].astype(jnp.float32), key_absorb.astype(jnp.float32)).astype(jnp.bfloat16)
    queries = jnp.concatenate([absorbed, projected[:, :, NOPE:]], axis=-1)
    index_queries = jnp.einsum('rq,qnd->rnd', latent.astype(jnp.float32), index_query.astype(jnp.float32)).astype(jnp.bfloat16)
    positions = jnp.arange(CTX, dtype=jnp.int32)

    def index_row(inputs):
        row_queries, row_keys, row_gate, row_length = inputs
        logits = jnp.dot(row_queries.astype(jnp.float32), row_keys.astype(jnp.float32).T, precision=lax.Precision.HIGHEST)
        score = lax.optimization_barrier(jnp.sum(row_gate[:, None] * jnp.maximum(logits, 0.0), axis=0)) * IDIM ** (-0.5)
        return jnp.where(positions < row_length, score, 0.0)
    index_scores = lax.map(index_row, (index_queries, index_keys, head_gate, lengths))

    def shard_part(shard):
        begin = shard * CTX_DEV
        cache = lax.dynamic_slice_in_dim(latent_cache, begin, CTX_DEV, 1).astype(jnp.float32)
        local_pos = begin + jnp.arange(CTX_DEV, dtype=jnp.int32)
        chosen = jnp.any(block_list[:, :, None] == (local_pos // BLK)[None, None, :], axis=1)
        live = chosen & (local_pos[None, :] < lengths[:, None])
        logits = jnp.einsum('rnc,rtc->rnt', queries.astype(jnp.float32), cache) * (NOPE + ROPE) ** (-0.5)
        masked = jnp.where(live[:, None, :], logits, very_low)
        peak = lax.optimization_barrier(jnp.max(masked, axis=-1))
        weights = jnp.where(live[:, None, :], jnp.exp(masked - peak[..., None]), 0.0)
        total = lax.optimization_barrier(jnp.sum(weights, axis=-1))
        rounded = lax.optimization_barrier(weights.astype(jnp.bfloat16)).astype(jnp.float32)
        output = jnp.einsum('rnt,rtc->rnc', rounded, cache[:, :, :KVLORA])
        return (peak, total, output)
    peaks, totals, outputs = lax.map(shard_part, jnp.arange(N_CTX, dtype=jnp.int32))
    highest = lax.optimization_barrier(jnp.max(peaks, axis=0))
    factor = jnp.exp(peaks - highest[None])
    total = lax.optimization_barrier(jnp.sum(totals * factor, axis=0))
    merged = lax.optimization_barrier(jnp.sum(outputs * factor[..., None], axis=0))
    attended = (merged / total[..., None]).astype(jnp.bfloat16)
    attn_out = jnp.einsum('rnc,ncv->rnv', attended.astype(jnp.float32), value_up.astype(jnp.float32)).astype(jnp.bfloat16)
    return (hidden, index_scores, attn_out)
```

```python
import functools

import jax
import jax.numpy as jnp
from jax import lax
from jax.experimental import pallas as pl
from jax.experimental.pallas import tpu as pltpu
from jax.sharding import PartitionSpec as P

D = 7168
KVLORA = 512
ROPE = 64
NOPE = 128
IHEADS = 64
IDIM = 128
BLK = 64


epsilon = 1e-06
very_low = -1e30


def shifted(size, step):
    return [(i, (i + step) % size) for i in range(size)]


def swapped(size, bit):
    return [(i, i ^ bit) for i in range(size)]


def pick_blocks(half, first_ref, row_ref, blocks_ref, cache_ref, keep_ref, send_ref):
    row = row_ref[0]
    width = cache_ref.shape[1]
    lane = lax.broadcasted_iota(jnp.int32, (width, 2 * BLK), 1)
    for j, out_ref in enumerate((keep_ref, send_ref)):
        begin = first_ref[1 + j]
        for pair in range(half // 2):
            total = jnp.zeros((width, 2 * BLK), jnp.float32)
            for side in range(2):
                local = blocks_ref[row, begin + 2 * pair + side] - first_ref[0]
                owned = (local >= 0) & (local < cache_ref.shape[2] // BLK)
                local = jnp.where(owned, local, 0)
                tile = cache_ref[row, :, pl.ds(pl.multiple_of(local // 2 * (2 * BLK), 2 * BLK), 2 * BLK)]
                tile = tile.astype(jnp.float32)
                swap = (local % 2) != side
                tile = jnp.where(swap, pltpu.roll(tile, BLK, 1), tile)
                mask = (lane // BLK == side) & owned
                total = jnp.where(mask, tile, total)
            out_ref[:, pair * 2 * BLK : (pair + 1) * 2 * BLK] = total.astype(out_ref.dtype)


def local(
    residual,
    expert_out,
    combine_slot,
    combine_gate,
    attn_gain,
    query_down,
    index_gate,
    latent_gain,
    query_up,
    key_absorb,
    index_query,
    value_up,
    latent_cache,
    index_keys,
    lengths,
    block_list,
):
    n_ctx, n_dp, n_hp = (lax.axis_size(name) for name in ("ctx", "dp", "hp"))
    c, d, h = (lax.axis_index(name) for name in ("ctx", "dp", "hp"))
    capacity = expert_out.shape[2]
    selected = block_list.shape[1]
    half = selected // 2
    span = latent_cache.shape[1]

    pieces = [(d, lax.dynamic_index_in_dim(expert_out[0], d, 0, False))]
    for step in range(1, n_dp):
        piece = lax.dynamic_index_in_dim(expert_out[0], (d + step) % n_dp, 0, False)
        pieces.append(((d + n_dp - step) % n_dp, lax.ppermute(piece, "dp", shifted(n_dp, step))))

    parity = c % 2
    first = jnp.stack([c * (span // BLK), parity * half, (1 - parity) * half]).astype(jnp.int32)
    width = latent_cache.shape[2]
    buffer = jax.ShapeDtypeStruct((width, half * BLK), jnp.bfloat16)
    smem = pl.BlockSpec(memory_space=pltpu.SMEM)
    vmem = pl.BlockSpec(memory_space=pltpu.VMEM)
    keep, send = pl.pallas_call(
        functools.partial(pick_blocks, half),
        out_shape=(buffer, buffer),
        in_specs=[smem, smem, smem, vmem],
        out_specs=(vmem, vmem),
        name="pick_blocks",
    )(first, h.reshape(1), block_list, jnp.swapaxes(latent_cache, 1, 2))
    held = keep + lax.ppermute(send, "ctx", swapped(n_ctx, 1))
    bit = 2
    while bit < n_ctx:
        held = held + lax.ppermute(held, "ctx", swapped(n_ctx, bit))
        bit *= 2
    other = lax.ppermute(held, "ctx", swapped(n_ctx, 1))
    mine = jnp.concatenate([held, other], axis=1)
    theirs = lax.ppermute(mine, "hp", swapped(n_hp, 1))

    routed = 0.0
    for source, piece in pieces:
        slot = source * capacity + jnp.arange(capacity, dtype=jnp.int32)
        weight = jnp.sum(
            jnp.where(combine_slot[:, :, None] == slot[None, None, :], combine_gate[:, :, None], 0.0), axis=1
        )
        routed = routed + jnp.sum(weight[:, :, None] * piece.astype(jnp.float32)[None], axis=1)
    hidden = (residual.astype(jnp.float32) + routed).astype(jnp.bfloat16)
    widened = hidden.astype(jnp.float32)
    scaled = (widened * attn_gain).astype(jnp.bfloat16)
    squares = jnp.sum(widened * widened, axis=1, keepdims=True)
    latent_part = jnp.dot(scaled, query_down, preferred_element_type=jnp.float32)
    gate_part = jnp.dot(scaled, index_gate, preferred_element_type=jnp.float32)
    part = jnp.concatenate([latent_part, gate_part, jnp.broadcast_to(squares, gate_part.shape)], axis=1)

    total = part
    for step in range(1, n_ctx):
        total = total + lax.ppermute(part, "ctx", shifted(n_ctx, step))
    qlora = latent_part.shape[1]
    scale = lax.rsqrt(total[:, qlora + IHEADS : qlora + IHEADS + 1] / D + epsilon)
    latent_sum = total[:, :qlora] * scale
    head_gate = total[:, qlora : qlora + IHEADS] * (scale * IHEADS**-0.5 * IDIM**-0.5)
    latent_scale = lax.rsqrt(jnp.mean(latent_sum * latent_sum, axis=-1, keepdims=True) + epsilon)
    latent = (latent_sum * latent_scale * latent_gain).astype(jnp.bfloat16)

    index_local = jnp.einsum("rq,qnd->nrd", latent, index_query, preferred_element_type=jnp.float32).astype(
        jnp.bfloat16
    )
    index_pair = lax.ppermute(index_local, "hp", swapped(n_hp, 1))
    index_pair = jnp.where(h == 0, jnp.stack([index_local, index_pair]), jnp.stack([index_pair, index_local]))
    gathered = [(c, index_pair)]
    for step in range(1, n_ctx):
        gathered.append(((c + n_ctx - step) % n_ctx, lax.ppermute(index_pair, "ctx", shifted(n_ctx, step))))
    gate_heads = head_gate.reshape(head_gate.shape[0], n_ctx, n_hp, -1)
    raw = 0.0
    for source, pair in gathered:
        gates = lax.dynamic_index_in_dim(gate_heads, source, 1, False)
        logits = jnp.einsum("hnrd,rtd->rhnt", pair, index_keys, preferred_element_type=jnp.float32)
        raw = raw + jnp.sum(gates[..., None] * jnp.maximum(logits, 0.0), axis=(1, 2))
    index_span = index_keys.shape[1]
    index_pos = (c * n_hp + h) * index_span + jnp.arange(index_span, dtype=jnp.int32)
    index_scores = jnp.where(index_pos[None, :] < lengths[:, None], raw, 0.0)

    projected = jnp.einsum("rq,qnd->rnd", latent, query_up, preferred_element_type=jnp.float32).astype(jnp.bfloat16)
    absorbed = jnp.einsum(
        "rnk,nkc->rnc", projected[:, :, :NOPE], key_absorb, preferred_element_type=jnp.float32
    ).astype(jnp.bfloat16)
    queries = jnp.concatenate([absorbed, projected[:, :, NOPE:]], axis=-1)
    cache = jnp.where(h == 0, jnp.stack([mine, theirs]), jnp.stack([theirs, mine]))
    order = jnp.where(parity == 0, block_list, jnp.concatenate([block_list[:, half:], block_list[:, :half]], axis=1))
    position = (order[:, :, None] * BLK + jnp.arange(BLK, dtype=jnp.int32)).reshape(order.shape[0], -1)
    live = (position < lengths[:, None])[:, None, :]
    logits = jnp.einsum("rnc,rct->rnt", queries, cache, preferred_element_type=jnp.float32) * (NOPE + ROPE) ** -0.5
    masked = jnp.where(live, logits, very_low)
    weights = jnp.where(live, jnp.exp(masked - jnp.max(masked, axis=-1, keepdims=True)), 0.0)
    merged = jnp.einsum(
        "rnt,rct->rnc", weights.astype(jnp.bfloat16), cache[:, :KVLORA], preferred_element_type=jnp.float32
    )
    attended = (merged / jnp.sum(weights, axis=-1, keepdims=True)).astype(jnp.bfloat16)
    attn_out = jnp.einsum("rnc,ncv->rnv", attended, value_up, preferred_element_type=jnp.float32).astype(jnp.bfloat16)
    return (hidden, index_scores, attn_out)


def solution(mesh):
    placed = (
        P(("groups", "dp"), "ctx"),
        P(("groups", "dp"), None, None, "ctx"),
        P(("groups", "dp"), None),
        P(("groups", "dp"), None),
        P("ctx"),
        P("ctx", None),
        P("ctx", None),
        P(),
        P(None, ("ctx", "hp"), None),
        P(("ctx", "hp"), None, None),
        P(None, ("ctx", "hp"), None),
        P(("ctx", "hp"), None, None),
        P(("groups", "dp"), "ctx", None),
        P(("groups", "dp"), ("ctx", "hp"), None),
        P(("groups", "dp")),
        P(("groups", "dp"), None),
    )
    return jax.shard_map(
        local,
        mesh=mesh,
        in_specs=placed,
        out_specs=(
            P(("groups", "dp"), "ctx"),
            P(("groups", "dp"), ("ctx", "hp")),
            P(("groups", "dp"), ("ctx", "hp"), None),
        ),
        check_vma=False,
    )
```

```python
import functools

import jax
import jax.numpy as jnp
from jax import lax
from jax.experimental import pallas as pl
from jax.experimental.pallas import tpu as pltpu
from jax.sharding import PartitionSpec as P

D = 7168
KVLORA = 512
ROPE = 64
NOPE = 128
IHEADS = 64
IDIM = 128
BLK = 64
LANES = 128


epsilon = 1e-06
very_low = -1e30

SMEM = pl.BlockSpec(memory_space=pltpu.SMEM)
VMEM = pl.BlockSpec(memory_space=pltpu.VMEM)
HBM = pl.BlockSpec(memory_space=pltpu.HBM)
NT = (((1,), (1,)), ((), ()))


def shifted(size, step):
    return [(i, (i + step) % size) for i in range(size)]


def swapped(size, bit):
    return [(i, i ^ bit) for i in range(size)]


def limits(mib):
    return pltpu.CompilerParams(vmem_limit_bytes=mib << 20)


def cost(mib):
    return pl.CostEstimate(flops=0, bytes_accessed=mib << 20, transcendentals=0)


def in_hbm(array):
    return pltpu.with_memory_space_constraint(array, pltpu.HBM)


def in_vmem(array):
    return pltpu.with_memory_space_constraint(array, pltpu.VMEM)


def prepare(
    first_ref, blocks_ref, cache_ref, slots_ref, down_ref, out_ref, own_ref, down_out_ref, tiles, sems, own_sem, down_sem
):
    own_copy = pltpu.make_async_copy(slots_ref.at[first_ref[2]], own_ref, own_sem)
    down_copy = pltpu.make_async_copy(down_ref, down_out_ref, down_sem)
    row = first_ref[0]
    width = cache_ref.shape[1]
    count = tiles.shape[0]
    spot = []
    for slot in range(count):
        local = blocks_ref[row, slot] - first_ref[1]
        owned = (local >= 0) & (local < cache_ref.shape[2] // BLK)
        local = jnp.where(owned, local, 0)
        begin = pl.multiple_of(local // 2 * LANES, LANES)
        copy = pltpu.make_async_copy(cache_ref.at[row, :, pl.ds(begin, LANES)], tiles.at[slot], sems.at[slot])
        copy.start()
        spot.append((copy, owned, (local % 2) != (slot % 2)))
    own_copy.start()
    down_copy.start()
    lane = lax.broadcasted_iota(jnp.int32, (width, LANES), 1)
    for pair in range(count // 2):
        total = jnp.zeros((width, LANES), jnp.float32)
        for side in range(2):
            copy, owned, swap = spot[2 * pair + side]
            copy.wait()
            tile = tiles[2 * pair + side].astype(jnp.float32)
            tile = jnp.where(swap, pltpu.roll(tile, BLK, 1), tile)
            total = jnp.where((lane // BLK == side) & owned, tile, total)
        out_ref[:, pair * LANES : (pair + 1) * LANES] = total.astype(out_ref.dtype)
    own_copy.wait()
    down_copy.wait()


def combine_down(
    sources, group_ref, slot_ref, gate_ref, residual_ref, gain_ref, own_ref, *refs
):
    received = refs[:sources]
    down_ref, igate_ref, hidden_ref, part_ref = refs[sources:]
    rows, features = residual_ref.shape
    capacity = own_ref.shape[0]
    group = group_ref[0]
    place = lax.broadcasted_iota(jnp.int32, (capacity, 1), 0)
    routed = [jnp.zeros((1, features), jnp.float32)] * rows
    for step, ref in enumerate((own_ref, *received)):
        source = lax.rem(group + len(received) + 1 - step, len(received) + 1)
        piece = (ref[...] if step == 0 else ref[pl.ds(group, 1)][0]).astype(jnp.float32)
        for r in range(rows):
            weight = jnp.zeros((capacity, 1), jnp.float32)
            for k in range(slot_ref.shape[1]):
                weight = weight + jnp.where(place == slot_ref[r, k] - source * capacity, gate_ref[r, k], 0.0)
            routed[r] = routed[r] + jnp.sum(weight * piece, axis=0, keepdims=True)
    hidden = (residual_ref[...].astype(jnp.float32) + jnp.concatenate(routed, axis=0)).astype(jnp.bfloat16)
    hidden_ref[...] = hidden
    widened = hidden.astype(jnp.float32)
    scaled = (widened * gain_ref[...]).astype(jnp.bfloat16)
    qlora = down_ref.shape[1]
    squares = jnp.sum(widened * widened, axis=1, keepdims=True)
    part_ref[:, qlora + LANES :] = jnp.broadcast_to(squares, (rows, LANES))
    gates = lax.dot_general(scaled, igate_ref[...], NT, preferred_element_type=jnp.float32)
    part_ref[:, qlora : qlora + LANES] = jnp.concatenate([gates, gates], axis=1)
    part_ref[:, :qlora] = jnp.dot(scaled, down_ref[...], preferred_element_type=jnp.float32)


def attend(
    first_ref, blocks_ref, lengths_ref, latent_ref, mine_ref, theirs_ref, up_ref, absorb_ref, value_ref, out_ref,
    up, absorb, value, absorbed, rotary, up_sem, absorb_sem, value_sem,
):
    heads = up_ref.shape[0]
    up_copies, absorb_copies = [], []
    for n in range(heads):
        up_copies.append(pltpu.make_async_copy(up_ref.at[n], up.at[n], up_sem.at[n]))
        up_copies[-1].start()
        absorb_copies.append(pltpu.make_async_copy(absorb_ref.at[n], absorb.at[n], absorb_sem.at[n]))
        absorb_copies[-1].start()
    value_copy = pltpu.make_async_copy(value_ref, value, value_sem)
    value_copy.start()
    latent = latent_ref[...]
    rows = latent.shape[0]
    for n in range(heads):
        up_copies[n].wait()
        projected = lax.dot_general(latent, up[n], NT, preferred_element_type=jnp.float32).astype(jnp.bfloat16)
        absorb_copies[n].wait()
        query = jnp.dot(projected[:, :NOPE], absorb[n], preferred_element_type=jnp.float32)
        for r in range(rows):
            absorbed[r, n : n + 1, :] = query[r : r + 1]
            rotary[r, n : n + 1, :] = projected[r : r + 1, NOPE:].astype(jnp.float32)
    this = first_ref[0]
    shape = (1, mine_ref.shape[1])
    lane = lax.broadcasted_iota(jnp.int32, shape, 1)
    attended = []
    for row, cache_ref in ((this, mine_ref), (1 - this, theirs_ref)):
        position = lane % BLK
        for slot in range(blocks_ref.shape[1]):
            position = position + jnp.where(lane // BLK == slot, blocks_ref[row, slot] * BLK, 0)
        live = position < lengths_ref[row]
        cache = cache_ref[...]
        logits = jnp.dot(
            absorbed[pl.ds(row, 1)][0].astype(jnp.bfloat16), cache[:KVLORA], preferred_element_type=jnp.float32
        ) + jnp.dot(rotary[pl.ds(row, 1)][0].astype(jnp.bfloat16), cache[KVLORA:], preferred_element_type=jnp.float32)
        masked = jnp.where(live, logits * (NOPE + ROPE) ** -0.5, very_low)
        weights = jnp.where(live, jnp.exp(masked - jnp.max(masked, axis=1, keepdims=True)), 0.0)
        total = jnp.sum(weights, axis=1, keepdims=True)
        merged = lax.dot_general(
            weights.astype(jnp.bfloat16), cache[:KVLORA], NT, preferred_element_type=jnp.float32
        )
        attended.append(merged / total)
    attended = jnp.concatenate(attended, axis=0).astype(jnp.bfloat16)
    value_copy.wait()
    head = lax.broadcasted_iota(jnp.int32, (2 * heads, value_ref.shape[2]), 0) % heads
    result = jnp.zeros(head.shape, jnp.float32)
    for n in range(heads):
        product = jnp.dot(attended, value[n], preferred_element_type=jnp.float32)
        result = jnp.where(head == n, product, result)
    for k, row in enumerate((this, 1 - this)):
        out_ref[pl.ds(row, 1)] = result[k * heads : (k + 1) * heads].astype(out_ref.dtype)[None]


def score(pieces, first_ref, lengths_ref, gates_ref, keys_ref, *refs):
    gathered = refs[:pieces]
    out_ref, queries = refs[pieces:]
    heads = gathered[0].shape[1]
    order = lax.broadcasted_iota(jnp.int32, (IHEADS, IHEADS), 0)
    head = order
    rows, span = out_ref.shape
    for k, ref in enumerate(gathered):
        for side in range(2):
            spot = 2 * k + side
            begin = first_ref[1 + k] + jnp.where(first_ref[0] == side, 0, heads)
            head = jnp.where(order // heads == spot, begin + order % heads, head)
            for r in range(rows):
                queries[r, spot * heads : (spot + 1) * heads, :] = ref[side, :, r, :].astype(jnp.float32)
    base = first_ref[1 + pieces]
    position = base + lax.broadcasted_iota(jnp.int32, (1, span), 1)
    for r in range(rows):
        logits = lax.dot_general(
            queries[r].astype(jnp.bfloat16), keys_ref[r], NT, preferred_element_type=jnp.float32
        )
        gates = jnp.where(lax.broadcasted_iota(jnp.int32, head.shape, 1) == head, gates_ref[r : r + 1, :], 0.0)
        gates = jnp.sum(gates, axis=1, keepdims=True)
        raw = jnp.sum(gates * jnp.maximum(logits, 0.0), axis=0, keepdims=True)
        out_ref[r : r + 1, :] = jnp.where(position < lengths_ref[r], raw, 0.0)


def local(
    residual,
    expert_out,
    combine_slot,
    combine_gate,
    attn_gain,
    query_down,
    index_gate,
    latent_gain,
    query_up,
    key_absorb,
    index_query,
    value_up,
    latent_cache,
    index_keys,
    lengths,
    block_list,
):
    n_ctx, n_dp, n_hp = (lax.axis_size(name) for name in ("ctx", "dp", "hp"))
    c, d, h = (lax.axis_index(name) for name in ("ctx", "dp", "hp"))
    rows, features = residual.shape
    qlora = query_down.shape[1]
    selected = block_list.shape[1]
    span, width = latent_cache.shape[1:]
    heads = value_up.shape[0]
    f32, bf16 = jnp.float32, jnp.bfloat16

    slots = expert_out[0]
    received = [lax.ppermute(slots, "dp", shifted(n_dp, step)) for step in range(1, n_dp)]

    place = jnp.stack([h, c * (span // BLK), d]).astype(jnp.int32)
    mine, own, down = pl.pallas_call(
        prepare,
        out_shape=(
            pltpu.VMEM((width, selected * BLK), bf16),
            pltpu.VMEM(slots.shape[1:], bf16),
            pltpu.VMEM(query_down.shape, bf16),
        ),
        in_specs=[SMEM, SMEM, HBM, HBM, HBM],
        out_specs=(VMEM, VMEM, VMEM),
        scratch_shapes=[
            pltpu.VMEM((selected, width, LANES), bf16),
            pltpu.SemaphoreType.DMA((selected,)),
            pltpu.SemaphoreType.DMA,
            pltpu.SemaphoreType.DMA,
        ],
        compiler_params=limits(8),
        cost_estimate=cost(1),
        name="prepare",
    )(place, block_list, in_hbm(jnp.swapaxes(latent_cache, 1, 2)), in_hbm(slots), in_hbm(query_down))
    neighbour = lax.ppermute(mine, "ctx", swapped(n_ctx, 1))
    received, mine = lax.optimization_barrier((received, mine))

    hidden, part = pl.pallas_call(
        functools.partial(combine_down, len(received)),
        out_shape=(
            jax.ShapeDtypeStruct((rows, features), bf16),
            pltpu.VMEM((rows, qlora + 2 * LANES), f32),
        ),
        in_specs=[SMEM] * 3 + [VMEM] * (5 + len(received)),
        out_specs=(VMEM, VMEM),
        compiler_params=limits(8),
        cost_estimate=cost(64),
        name="combine_down",
    )(
        d.reshape(1).astype(jnp.int32), combine_slot, combine_gate, residual, attn_gain.reshape(1, -1), in_vmem(own),
        *received, in_vmem(down), index_gate.T,
    )

    mine, part = lax.optimization_barrier((mine + neighbour, part))
    bit = 2
    while bit < n_ctx:
        mine = mine + lax.ppermute(mine, "ctx", swapped(n_ctx, bit))
        bit *= 2

    total = part
    for step in range(1, n_ctx):
        total = total + lax.ppermute(part, "ctx", swapped(n_ctx, step))
    scale = lax.rsqrt(total[:, qlora + LANES : qlora + LANES + 1] / D + epsilon)
    latent_sum = total[:, :qlora] * scale
    head_gate = total[:, qlora : qlora + IHEADS] * (scale * IHEADS**-0.5 * IDIM**-0.5)
    latent_scale = lax.rsqrt(jnp.mean(latent_sum * latent_sum, axis=-1, keepdims=True) + epsilon)
    latent = (latent_sum * latent_scale * latent_gain).astype(bf16)

    index_local = jnp.einsum("rq,qnd->nrd", latent, index_query, preferred_element_type=f32).astype(bf16)
    index_pair = jnp.stack([index_local, lax.ppermute(index_local, "hp", swapped(n_hp, 1))])
    gathered = [index_pair] + [lax.ppermute(index_pair, "ctx", swapped(n_ctx, step)) for step in range(1, n_ctx)]
    index_heads, index_span = index_local.shape[0], index_keys.shape[1]
    sources = [jnp.bitwise_xor(c, step) * n_hp * index_heads for step in range(n_ctx)]
    theirs = lax.ppermute(mine, "hp", swapped(n_hp, 1))
    latent, index_pair = lax.optimization_barrier((latent, index_pair))
    attn_out = pl.pallas_call(
        attend,
        out_shape=jax.ShapeDtypeStruct((rows, heads, value_up.shape[2]), bf16),
        in_specs=[SMEM, SMEM, SMEM, VMEM, VMEM, VMEM, HBM, HBM, HBM],
        out_specs=VMEM,
        scratch_shapes=[
            pltpu.VMEM((heads, query_up.shape[2], qlora), bf16),
            pltpu.VMEM(key_absorb.shape, bf16),
            pltpu.VMEM(value_up.shape, bf16),
            pltpu.VMEM((rows, heads, KVLORA), f32),
            pltpu.VMEM((rows, heads, ROPE), f32),
            pltpu.SemaphoreType.DMA((heads,)),
            pltpu.SemaphoreType.DMA((heads,)),
            pltpu.SemaphoreType.DMA,
        ],
        compiler_params=limits(24),
        cost_estimate=cost(14),
        name="attend",
    )(
        place, block_list, lengths, latent, mine, theirs, in_hbm(jnp.transpose(query_up, (1, 2, 0))),
        in_hbm(key_absorb), in_hbm(value_up),
    )
    gathered, attn_out = lax.optimization_barrier((gathered, attn_out))
    index_scores = pl.pallas_call(
        functools.partial(score, n_ctx),
        out_shape=jax.ShapeDtypeStruct((rows, index_span), f32),
        in_specs=[SMEM, SMEM, VMEM, VMEM] + [VMEM] * n_ctx,
        out_specs=VMEM,
        scratch_shapes=[pltpu.VMEM((rows, IHEADS, IDIM), f32)],
        compiler_params=limits(4),
        cost_estimate=cost(2),
        name="score",
    )(
        jnp.stack([h, *sources, (c * n_hp + h) * index_span]).astype(jnp.int32), lengths, head_gate, index_keys,
        *gathered,
    )

    return (hidden, index_scores, attn_out)

def solution(mesh):
    placed = (
        P(("groups", "dp"), "ctx"),
        P(("groups", "dp"), None, None, "ctx"),
        P(("groups", "dp"), None),
        P(("groups", "dp"), None),
        P("ctx"),
        P("ctx", None),
        P("ctx", None),
        P(),
        P(None, ("ctx", "hp"), None),
        P(("ctx", "hp"), None, None),
        P(None, ("ctx", "hp"), None),
        P(("ctx", "hp"), None, None),
        P(("groups", "dp"), "ctx", None),
        P(("groups", "dp"), ("ctx", "hp"), None),
        P(("groups", "dp")),
        P(("groups", "dp"), None),
    )
    return jax.shard_map(
        local,
        mesh=mesh,
        in_specs=placed,
        out_specs=(
            P(("groups", "dp"), "ctx"),
            P(("groups", "dp"), ("ctx", "hp")),
            P(("groups", "dp"), ("ctx", "hp"), None),
        ),
        check_vma=False,
    )
```

```python
import functools

import jax
import jax.numpy as jnp
from jax import lax
from jax.experimental import pallas as pl
from jax.experimental.pallas import tpu as pltpu
from jax.sharding import PartitionSpec as P

D = 7168
KVLORA = 512
ROPE = 64
NOPE = 128
IHEADS = 64
IDIM = 128
BLK = 64
LANES = 128


epsilon = 1e-06
very_low = -1e30

SMEM = pl.BlockSpec(memory_space=pltpu.SMEM)
VMEM = pl.BlockSpec(memory_space=pltpu.VMEM)
HBM = pl.BlockSpec(memory_space=pltpu.HBM)
NT = (((1,), (1,)), ((), ()))


def shifted(size, step):
    return [(i, (i + step) % size) for i in range(size)]


def swapped(size, bit):
    return [(i, i ^ bit) for i in range(size)]


def limits(mib):
    return pltpu.CompilerParams(vmem_limit_bytes=mib << 20)


def cost(mib):
    return pl.CostEstimate(flops=0, bytes_accessed=mib << 20, transcendentals=0)


def in_hbm(array):
    return pltpu.with_memory_space_constraint(array, pltpu.HBM)


def in_vmem(array):
    return pltpu.with_memory_space_constraint(array, pltpu.VMEM)


def pick_blocks(place, blocks_ref, cache_ref, keep_ref, send_ref, tiles, sems):
    row = place[0]
    width = cache_ref.shape[1]
    count = tiles.shape[0]
    spot = []
    for slot in range(count):
        local = blocks_ref[row, lax.rem(slot + place[2] * (count // 2), count)] - place[1]
        owned = (local >= 0) & (local < cache_ref.shape[2] // BLK)
        local = jnp.where(owned, local, 0)
        begin = pl.multiple_of(local // 2 * LANES, LANES)
        copy = pltpu.make_async_copy(cache_ref.at[row, :, pl.ds(begin, LANES)], tiles.at[slot], sems.at[slot])
        copy.start()
        spot.append((copy, owned, (local % 2) != (slot % 2)))
    lane = lax.broadcasted_iota(jnp.int32, (width, LANES), 1)
    for pair in range(count // 2):
        total = jnp.zeros((width, LANES), jnp.float32)
        for side in range(2):
            copy, owned, swap = spot[2 * pair + side]
            copy.wait()
            tile = tiles[2 * pair + side].astype(jnp.float32)
            tile = jnp.where(swap, pltpu.roll(tile, BLK, 1), tile)
            total = jnp.where((lane // BLK == side) & owned, tile, total)
        out_ref = keep_ref if 4 * pair < count else send_ref
        begin = pair % (count // 4) * LANES
        out_ref[:, begin : begin + LANES] = total.astype(out_ref.dtype)


def prepare(
    sources, place, blocks_ref, lengths_ref, slot_ref, gate_ref, slots_ref, residual_ref, gain_ref, igate_ref, down_ref,
    base_ref, weight_ref, live_ref, limit_ref, gain_out_ref, igate_out_ref, down_out_ref, own, residual, sems,
):
    this, group = place[0], place[3]
    moved = (
        (down_ref, down_out_ref), (slots_ref.at[group], own), (residual_ref, residual), (gain_ref, gain_out_ref),
        (igate_ref, igate_out_ref),
    )
    moves = [pltpu.make_async_copy(source, target, sems.at[k]) for k, (source, target) in enumerate(moved)]
    for move in moves:
        move.start()
    rows = residual.shape[0]
    count = blocks_ref.shape[1]
    lane = lax.broadcasted_iota(jnp.int32, (1, live_ref.shape[1]), 1)
    for k, row in enumerate((this, 1 - this)):
        position = lane % BLK
        for slot in range(count):
            block = blocks_ref[row, lax.rem(slot + place[2] * (count // 2), count)]
            position = position + jnp.where(lane // BLK == slot, block * BLK, 0)
        live_ref[k : k + 1, :] = (position < lengths_ref[row]).astype(jnp.float32)
    position = place[4] + lax.broadcasted_iota(jnp.int32, (1, limit_ref.shape[1]), 1)
    for r in range(rows):
        limit_ref[r : r + 1, :] = (position < lengths_ref[r]).astype(jnp.float32)
    capacity = own.shape[0]
    spot = lax.broadcasted_iota(jnp.int32, (capacity, LANES), 0)
    weights = []
    for step in range(sources + 1):
        source = lax.rem(group + sources + 1 - step, sources + 1)
        for r in range(rows):
            weight = jnp.zeros(spot.shape, jnp.float32)
            for k in range(slot_ref.shape[1]):
                weight = jnp.where(spot == slot_ref[r, k] - source * capacity, gate_ref[r, k], weight)
            if step == 0:
                weights.append(weight[:, :1])
            else:
                weight_ref[step - 1, r] = weight
    for move in moves[1:]:
        move.wait()
    for r in range(rows):
        routed = jnp.sum(weights[r] * own[...].astype(jnp.float32), axis=0, keepdims=True)
        base_ref[r : r + 1, :] = residual[r : r + 1].astype(jnp.float32) + routed
    moves[0].wait()


def combine_down(
    sources, place, base_ref, weight_ref, gain_ref, igate_ref, down_ref, *refs
):
    received = refs[:sources]
    hidden_ref, part_ref = refs[sources:]
    rows = base_ref.shape[0]
    group = place[3]
    routed = [base_ref[r : r + 1, :] for r in range(rows)]
    for k, ref in enumerate(received):
        piece = ref[pl.ds(group, 1)][0].astype(jnp.float32)
        for r in range(rows):
            routed[r] = routed[r] + jnp.sum(weight_ref[k, r][:, :1] * piece, axis=0, keepdims=True)
    hidden = jnp.concatenate(routed, axis=0).astype(jnp.bfloat16)
    hidden_ref[...] = hidden
    widened = hidden.astype(jnp.float32)
    scaled = (widened * gain_ref[...].reshape(1, -1)).astype(jnp.bfloat16)
    qlora = down_ref.shape[1]
    squares = jnp.sum(widened * widened, axis=1, keepdims=True)
    part_ref[:, qlora + LANES :] = jnp.broadcast_to(squares, (rows, LANES))
    gates = lax.dot_general(scaled, igate_ref[...], NT, preferred_element_type=jnp.float32)
    part_ref[:, qlora : qlora + LANES] = jnp.concatenate([gates, gates], axis=1)
    part_ref[:, :qlora] = jnp.dot(scaled, down_ref[...], preferred_element_type=jnp.float32)


def project(chunk, begin, latent_ref, up_ref, absorb_ref, *refs):
    extra = (len(refs) - 5) // 3
    later = refs[:extra]
    absorbed, rotary = refs[extra : extra + 2]
    brought = refs[extra + 2 : 2 * extra + 2]
    turned, up, sems = refs[2 * extra + 2 : 2 * extra + 5]
    heads = turned.shape[0]
    rows, qlora = latent_ref.shape
    copies = []
    for k in range(heads // chunk):
        span = pl.ds(k * chunk, chunk)
        copies.append(pltpu.make_async_copy(up_ref.at[pl.ds(begin + k * chunk, chunk)], up.at[span], sems.at[k]))
        copies[-1].start()
    moves = []
    for k in range(extra):
        moves.append(pltpu.make_async_copy(later[k], brought[k], refs[2 * extra + 5 + k]))
        moves[-1].start()
    column = latent_ref[...].astype(jnp.float32)
    column = jnp.concatenate([column, jnp.zeros((LANES - rows, qlora), jnp.float32)], axis=0)
    column = jnp.transpose(column).astype(jnp.bfloat16)
    for k, copy in enumerate(copies):
        copy.wait()
        for n in range(k * chunk, (k + 1) * chunk):
            turned[n] = jnp.dot(up[n], column, preferred_element_type=jnp.float32)
    for n in range(heads):
        projected = jnp.transpose(turned[n])[:rows].astype(jnp.bfloat16)
        query = jnp.dot(projected[:, :NOPE], absorb_ref[begin + n], preferred_element_type=jnp.float32)
        for r in range(rows):
            absorbed[r, n : n + 1, :] = query[r : r + 1].astype(jnp.bfloat16).astype(jnp.float32)
            rotary[r, n : n + 1, :] = projected[r : r + 1, NOPE:].astype(jnp.float32)
    for move in moves:
        move.wait()


def attend(place, live_ref, *refs):
    parts = (len(refs) - 4) // 2
    absorbed, rotary = refs[:parts], refs[parts : 2 * parts]
    mine_ref, theirs_ref, value_ref, out_ref = refs[2 * parts :]
    heads = value_ref.shape[0]
    this = place[0]
    attended = []
    for k, (row, cache_ref) in enumerate(((this, mine_ref), (1 - this, theirs_ref))):
        live = live_ref[k : k + 1, :] > 0.0
        cache = cache_ref[...]
        content = jnp.concatenate([ref[pl.ds(row, 1)][0] for ref in absorbed], axis=0).astype(jnp.bfloat16)
        turn = jnp.concatenate([ref[pl.ds(row, 1)][0] for ref in rotary], axis=0).astype(jnp.bfloat16)
        logits = jnp.dot(content, cache[:KVLORA], preferred_element_type=jnp.float32) + jnp.dot(
            turn, cache[KVLORA:], preferred_element_type=jnp.float32
        )
        masked = jnp.where(live, logits * (NOPE + ROPE) ** -0.5, very_low)
        weights = jnp.where(live, jnp.exp(masked - jnp.max(masked, axis=1, keepdims=True)), 0.0)
        total = jnp.sum(weights, axis=1, keepdims=True)
        merged = lax.dot_general(
            weights.astype(jnp.bfloat16), cache[:KVLORA], NT, preferred_element_type=jnp.float32
        )
        attended.append(merged / total)
    attended = jnp.concatenate(attended, axis=0).astype(jnp.bfloat16)
    head = lax.broadcasted_iota(jnp.int32, (2 * heads, value_ref.shape[2]), 0) % heads
    result = jnp.zeros(head.shape, jnp.float32)
    for n in range(heads):
        product = jnp.dot(attended, value_ref[n], preferred_element_type=jnp.float32)
        result = jnp.where(head == n, product, result)
    for k, row in enumerate((this, 1 - this)):
        out_ref[pl.ds(row, 1)] = result[k * heads : (k + 1) * heads].astype(out_ref.dtype)[None]


def score(pieces, place, limit_ref, gates_ref, keys_ref, *refs):
    gathered = refs[:pieces]
    out_ref, queries = refs[pieces:]
    heads = gathered[0].shape[1]
    order = lax.broadcasted_iota(jnp.int32, (IHEADS, IHEADS), 0)
    head = order
    rows = out_ref.shape[0]
    for k, ref in enumerate(gathered):
        for side in range(2):
            spot = 2 * k + side
            begin = place[5 + k] + jnp.where(place[0] == side, 0, heads)
            head = jnp.where(order // heads == spot, begin + order % heads, head)
            for r in range(rows):
                queries[r, spot * heads : (spot + 1) * heads, :] = ref[side, :, r, :].astype(jnp.float32)
    for r in range(rows):
        logits = lax.dot_general(
            queries[r].astype(jnp.bfloat16), keys_ref[r], NT, preferred_element_type=jnp.float32
        )
        gates = jnp.where(lax.broadcasted_iota(jnp.int32, head.shape, 1) == head, gates_ref[r : r + 1, :], 0.0)
        gates = jnp.sum(gates, axis=1, keepdims=True)
        raw = jnp.sum(gates * jnp.maximum(logits, 0.0), axis=0, keepdims=True)
        out_ref[r : r + 1, :] = jnp.where(limit_ref[r : r + 1, :] > 0.0, raw, 0.0)


def local(
    residual,
    expert_out,
    combine_slot,
    combine_gate,
    attn_gain,
    query_down,
    index_gate,
    latent_gain,
    query_up,
    key_absorb,
    index_query,
    value_up,
    latent_cache,
    index_keys,
    lengths,
    block_list,
):
    n_ctx, n_dp, n_hp = (lax.axis_size(name) for name in ("ctx", "dp", "hp"))
    c, d, h = (lax.axis_index(name) for name in ("ctx", "dp", "hp"))
    rows, features = residual.shape
    qlora = query_down.shape[1]
    selected = block_list.shape[1]
    span, width = latent_cache.shape[1:]
    heads = value_up.shape[0]
    f32, bf16 = jnp.float32, jnp.bfloat16

    slots = expert_out[0]
    received = [lax.ppermute(slots, "dp", shifted(n_dp, step)) for step in range(1, n_dp)]

    index_heads, index_span = index_query.shape[1], index_keys.shape[1]
    sources = [jnp.bitwise_xor(c, step) * n_hp * index_heads for step in range(n_ctx)]
    scalars = [h, c * (span // BLK), c % 2, d, (c * n_hp + h) * index_span, *sources]
    place = in_vmem(jnp.stack(scalars).astype(jnp.int32))
    half = pltpu.VMEM((width, selected // 2 * BLK), bf16)
    mine, send = pl.pallas_call(
        pick_blocks,
        out_shape=(half, half),
        in_specs=[SMEM, SMEM, HBM],
        out_specs=(VMEM, VMEM),
        scratch_shapes=[pltpu.VMEM((selected, width, LANES), bf16), pltpu.SemaphoreType.DMA((selected,))],
        compiler_params=limits(6),
        name="pick_blocks",
    )(place, in_hbm(block_list), in_hbm(jnp.swapaxes(latent_cache, 1, 2)))
    upper, lower = (lax.ppermute(x, "ctx", swapped(n_ctx, 1)) for x in (send[: width // 2], send[width // 2 :]))
    mine, residual = lax.optimization_barrier((mine, residual))
    *ready, live, limit, gain, igate, down = pl.pallas_call(
        functools.partial(prepare, len(received)),
        out_shape=(
            pltpu.VMEM((rows, features), f32),
            pltpu.VMEM((len(received), rows, slots.shape[1], LANES), f32),
            pltpu.VMEM((rows, selected * BLK), f32),
            pltpu.VMEM((rows, index_span), f32),
            pltpu.VMEM(attn_gain.shape, f32),
            pltpu.VMEM(index_gate.shape[::-1], bf16),
            pltpu.VMEM(query_down.shape, bf16),
        ),
        in_specs=[SMEM] * 5 + [HBM] * 5,
        out_specs=(VMEM,) * 7,
        scratch_shapes=[
            pltpu.VMEM(slots.shape[1:], bf16),
            pltpu.VMEM(residual.shape, bf16),
            pltpu.SemaphoreType.DMA((5,)),
        ],
        compiler_params=limits(4),
        name="prepare",
    )(
        place,
        *map(in_hbm, (block_list, lengths, combine_slot, combine_gate)),
        *map(in_hbm, (slots, residual, attn_gain, index_gate.T, query_down)),
    )
    ready = [*ready, gain, igate, down]
    received, ready = lax.optimization_barrier((received, ready))

    hidden, part = pl.pallas_call(
        functools.partial(combine_down, len(received)),
        out_shape=(
            jax.ShapeDtypeStruct((rows, features), bf16),
            pltpu.VMEM((rows, qlora + 2 * LANES), f32),
        ),
        in_specs=[SMEM] + [VMEM] * (5 + len(received)),
        out_specs=(VMEM, VMEM),
        compiler_params=limits(8),
        cost_estimate=cost(10),
        name="combine_down",
    )(place, *map(in_vmem, ready), *received)

    mine, upper, lower, part = lax.optimization_barrier((mine, upper, lower, part))
    mine = mine + jnp.concatenate([upper, lower], axis=0)
    mine, part = lax.optimization_barrier((mine, part))
    crossed = [lax.ppermute(mine, "ctx", swapped(n_ctx, 2))]

    parts = [part] + [lax.ppermute(part, "ctx", swapped(n_ctx, step)) for step in range(1, n_ctx)]
    total = functools.reduce(jnp.add, parts)
    scale = lax.rsqrt(total[:, qlora + LANES : qlora + LANES + 1] / D + epsilon)
    latent_sum = total[:, :qlora] * scale
    head_gate = total[:, qlora : qlora + IHEADS] * (scale * IHEADS**-0.5 * IDIM**-0.5)
    latent_scale = lax.rsqrt(jnp.mean(latent_sum * latent_sum, axis=-1, keepdims=True) + epsilon)
    latent = (latent_sum * latent_scale * latent_gain).astype(bf16)

    index_local = jnp.einsum("rq,qnd->nrd", latent, index_query, preferred_element_type=f32).astype(bf16)
    index_other = lax.ppermute(index_local, "hp", swapped(n_hp, 1))
    index_pair = jnp.stack([index_local, index_other])
    gathered = [index_pair] + [lax.ppermute(index_pair, "ctx", swapped(n_ctx, step)) for step in range(1, n_ctx)]

    def project_part(begin, count, latent, later):
        group = 2 if count % 2 == 0 else 1
        return pl.pallas_call(
            functools.partial(project, group, begin),
            out_shape=(
                pltpu.VMEM((rows, count, KVLORA), f32),
                pltpu.VMEM((rows, count, ROPE), f32),
                *(pltpu.VMEM(array.shape, array.dtype) for array in later),
            ),
            in_specs=[VMEM, HBM, VMEM] + [HBM] * len(later),
            out_specs=(VMEM,) * (2 + len(later)),
            scratch_shapes=[
                pltpu.VMEM((count, query_up.shape[2], LANES), f32),
                pltpu.VMEM((count, query_up.shape[2], qlora), bf16),
                pltpu.SemaphoreType.DMA((count // group,)),
                *(pltpu.SemaphoreType.DMA for _ in later),
            ],
            compiler_params=limits(10),
            name="project",
        )(in_vmem(latent), in_hbm(jnp.transpose(query_up, (1, 2, 0))), in_vmem(key_absorb), *map(in_hbm, later))

    lead = max(1, heads * 3 // 4)
    latent, index_pair = lax.optimization_barrier((latent, index_pair))
    first = project_part(0, lead, latent, ())
    first, mine, crossed, gathered = lax.optimization_barrier((first, mine, crossed, gathered))
    mine = functools.reduce(jnp.add, crossed, mine)
    bit = 4
    while bit < n_ctx:
        mine = mine + lax.ppermute(mine, "ctx", swapped(n_ctx, bit))
        bit *= 2
    mine, latent = lax.optimization_barrier((mine, latent))
    other = lax.ppermute(mine, "ctx", swapped(n_ctx, 1))
    *second, value, keys = project_part(lead, heads - lead, latent, (value_up, index_keys))
    second, mine, other = lax.optimization_barrier((second, mine, other))
    mine = jnp.concatenate([mine, other], axis=1)
    theirs = lax.ppermute(mine, "hp", swapped(n_hp, 1))
    index_scores = pl.pallas_call(
        functools.partial(score, n_ctx),
        out_shape=jax.ShapeDtypeStruct((rows, index_span), f32),
        in_specs=[SMEM] + [VMEM] * (3 + n_ctx),
        out_specs=VMEM,
        scratch_shapes=[pltpu.VMEM((rows, IHEADS, IDIM), f32)],
        compiler_params=limits(4),
        cost_estimate=cost(2),
        name="score",
    )(place, *map(in_vmem, (limit, head_gate, keys, *gathered)))

    index_scores, mine = lax.optimization_barrier((index_scores, mine))
    attn_out = pl.pallas_call(
        attend,
        out_shape=jax.ShapeDtypeStruct((rows, heads, value_up.shape[2]), bf16),
        in_specs=[SMEM] + [VMEM] * 8,
        out_specs=VMEM,
        compiler_params=limits(8),
        name="attend",
    )(place, *map(in_vmem, (live, first[0], second[0], first[1], second[1], mine, theirs, value)))
    return (hidden, index_scores, attn_out)


def solution(mesh):
    placed = (
        P(("groups", "dp"), "ctx"),
        P(("groups", "dp"), None, None, "ctx"),
        P(("groups", "dp"), None),
        P(("groups", "dp"), None),
        P("ctx"),
        P("ctx", None),
        P("ctx", None),
        P(),
        P(None, ("ctx", "hp"), None),
        P(("ctx", "hp"), None, None),
        P(None, ("ctx", "hp"), None),
        P(("ctx", "hp"), None, None),
        P(("groups", "dp"), "ctx", None),
        P(("groups", "dp"), ("ctx", "hp"), None),
        P(("groups", "dp")),
        P(("groups", "dp"), None),
    )
    return jax.shard_map(
        local,
        mesh=mesh,
        in_specs=placed,
        out_specs=(
            P(("groups", "dp"), "ctx"),
            P(("groups", "dp"), ("ctx", "hp")),
            P(("groups", "dp"), ("ctx", "hp"), None),
        ),
        check_vma=False,
    )
```

```python
import functools

import jax
import jax.numpy as jnp
from jax import lax
from jax.experimental import pallas as pl
from jax.experimental.pallas import tpu as pltpu
from jax.sharding import PartitionSpec as P

D = 7168
KVLORA = 512
ROPE = 64
NOPE = 128
IHEADS = 64
IDIM = 128
BLK = 64
LANES = 128


epsilon = 1e-06
very_low = -1e30

SMEM = pl.BlockSpec(memory_space=pltpu.SMEM)
VMEM = pl.BlockSpec(memory_space=pltpu.VMEM)
HBM = pl.BlockSpec(memory_space=pltpu.HBM)
NT = (((1,), (1,)), ((), ()))


def shifted(size, step):
    return [(i, (i + step) % size) for i in range(size)]


def swapped(size, bit):
    return [(i, i ^ bit) for i in range(size)]


def limits(mib):
    return pltpu.CompilerParams(vmem_limit_bytes=mib << 20)


def in_hbm(array):
    return pltpu.with_memory_space_constraint(array, pltpu.HBM)


def in_vmem(array):
    return pltpu.with_memory_space_constraint(array, pltpu.VMEM)


def prepare(
    sources, place, blocks_hbm, lengths_hbm, slot_hbm, gate_hbm, cache_ref, slots_ref, residual_ref, gain_ref, igate_ref, down_ref,
    keep_ref, send_ref, base_ref, weight_ref, live_ref, limit_ref, gain_out_ref, igate_out_ref, down_out_ref,
    blocks_ref, lengths_ref, slot_ref, gate_ref, cache, own, residual, scalar_sems, sems,
):
    this, group = place[0], place[3]
    width = cache_ref.shape[1]
    count = blocks_hbm.shape[1]
    scalars = ((blocks_hbm, blocks_ref), (lengths_hbm, lengths_ref), (slot_hbm, slot_ref), (gate_hbm, gate_ref))
    fetched = [pltpu.make_async_copy(source, target, scalar_sems.at[k]) for k, (source, target) in enumerate(scalars)]
    for copy in fetched:
        copy.start()
    moved = (
        (down_ref, down_out_ref), (cache_ref.at[this], cache), (slots_ref.at[group], own), (residual_ref, residual), (gain_ref, gain_out_ref),
        (igate_ref, igate_out_ref),
    )
    moves = [pltpu.make_async_copy(source, target, sems.at[k]) for k, (source, target) in enumerate(moved)]
    for move in (*moves[1:], moves[0]):
        move.start()
    for copy in fetched:
        copy.wait()
    spots = []
    for slot in range(count):
        local = blocks_ref[this, lax.rem(slot + place[2] * (count // 2), count)] - place[1]
        owned = (local >= 0) & (local < cache_ref.shape[2] // BLK)
        local = jnp.where(owned, local, 0)
        begin = pl.multiple_of(local // 2 * LANES, LANES)
        spots.append((begin, owned, (local % 2) != (slot % 2)))
    rows = residual.shape[0]
    lane = lax.broadcasted_iota(jnp.int32, (1, live_ref.shape[1]), 1)
    for k, row in enumerate((this, 1 - this)):
        position = lane % BLK
        for slot in range(count):
            block = blocks_ref[row, lax.rem(slot + place[2] * (count // 2), count)]
            position = position + jnp.where(lane // BLK == slot, block * BLK, 0)
        live_ref[k : k + 1, :] = (position < lengths_ref[row]).astype(jnp.float32)
    position = place[4] + lax.broadcasted_iota(jnp.int32, (1, limit_ref.shape[1]), 1)
    for r in range(rows):
        limit_ref[r : r + 1, :] = (position < lengths_ref[r]).astype(jnp.float32)
    capacity = own.shape[0]
    spot = lax.broadcasted_iota(jnp.int32, (capacity, LANES), 0)
    weights = []
    for step in range(sources + 1):
        source = lax.rem(group + sources + 1 - step, sources + 1)
        for r in range(rows):
            weight = jnp.zeros(spot.shape, jnp.float32)
            for k in range(slot_ref.shape[1]):
                weight = jnp.where(spot == slot_ref[r, k] - source * capacity, gate_ref[r, k], weight)
            if step == 0:
                weights.append(weight[:, :1])
            else:
                weight_ref[step - 1, r] = weight
    moves[1].wait()
    lane = lax.broadcasted_iota(jnp.int32, (width, LANES), 1)
    for pair in range(count // 2):
        total = jnp.zeros((width, LANES), jnp.float32)
        for side in range(2):
            begin, owned, swap = spots[2 * pair + side]
            tile = cache[:, pl.ds(begin, LANES)].astype(jnp.float32)
            tile = jnp.where(swap, pltpu.roll(tile, BLK, 1), tile)
            total = jnp.where((lane // BLK == side) & owned, tile, total)
        out_ref = keep_ref if 4 * pair < count else send_ref
        begin = pair % (count // 4) * LANES
        out_ref[:, begin : begin + LANES] = total.astype(out_ref.dtype)
    for move in moves[2:]:
        move.wait()
    for r in range(rows):
        routed = jnp.sum(weights[r] * own[...].astype(jnp.float32), axis=0, keepdims=True)
        base_ref[r : r + 1, :] = residual[r : r + 1].astype(jnp.float32) + routed
    moves[0].wait()


def combine_down(
    sources, place, base_ref, weight_ref, gain_ref, igate_ref, down_ref, *refs
):
    received = refs[:sources]
    hidden_ref, part_ref = refs[sources:]
    rows = base_ref.shape[0]
    group = place[3]
    routed = [base_ref[r : r + 1, :] for r in range(rows)]
    for k, ref in enumerate(received):
        piece = ref[pl.ds(group, 1)][0].astype(jnp.float32)
        for r in range(rows):
            routed[r] = routed[r] + jnp.sum(weight_ref[k, r][:, :1] * piece, axis=0, keepdims=True)
    hidden = jnp.concatenate(routed, axis=0).astype(jnp.bfloat16)
    hidden_ref[...] = hidden
    widened = hidden.astype(jnp.float32)
    scaled = (widened * gain_ref[...].reshape(1, -1)).astype(jnp.bfloat16)
    qlora = down_ref.shape[1]
    squares = jnp.sum(widened * widened, axis=1, keepdims=True)
    part_ref[:, qlora + LANES :] = jnp.broadcast_to(squares, (rows, LANES))
    gates = lax.dot_general(scaled, igate_ref[...], NT, preferred_element_type=jnp.float32)
    part_ref[:, qlora : qlora + LANES] = jnp.concatenate([gates, gates], axis=1)
    part_ref[:, :qlora] = jnp.dot(scaled, down_ref[...], preferred_element_type=jnp.float32)


def attend_row(live, content, turn, cache):
    logits = jnp.dot(content, cache[:KVLORA], preferred_element_type=jnp.float32) + jnp.dot(
        turn, cache[KVLORA:], preferred_element_type=jnp.float32
    )
    masked = jnp.where(live, logits * (NOPE + ROPE) ** -0.5, very_low)
    weights = jnp.where(live, jnp.exp(masked - jnp.max(masked, axis=1, keepdims=True)), 0.0)
    total = jnp.sum(weights, axis=1, keepdims=True)
    merged = lax.dot_general(weights.astype(jnp.bfloat16), cache[:KVLORA], NT, preferred_element_type=jnp.float32)
    return merged / total


def attend_first(place, live_ref, absorbed, rotary, cache_ref, out_ref):
    row = place[0]
    live = live_ref[:1, :] > 0.0
    out_ref[...] = attend_row(live, absorbed[pl.ds(row, 1)][0], rotary[pl.ds(row, 1)][0], cache_ref[...])


def finish(
    pieces, place, live_ref, absorbed, rotary, first_ref, cache_ref, value_ref, limit_ref, gates_ref, keys_ref, *refs
):
    gathered = refs[:pieces]
    out_ref, scores_ref, queries = refs[pieces:]
    index_heads = gathered[0].shape[1]
    order = lax.broadcasted_iota(jnp.int32, (IHEADS, IHEADS), 0)
    head = order
    for k, ref in enumerate(gathered):
        for side in range(2):
            spot = 2 * k + side
            begin = place[5 + k] + jnp.where(place[0] == side, 0, index_heads)
            head = jnp.where(order // index_heads == spot, begin + order % index_heads, head)
            for r in range(scores_ref.shape[0]):
                queries[r, spot * index_heads : (spot + 1) * index_heads, :] = ref[side, :, r, :].astype(jnp.float32)
    for r in range(scores_ref.shape[0]):
        logits = lax.dot_general(
            queries[r].astype(jnp.bfloat16), keys_ref[r], NT, preferred_element_type=jnp.float32
        )
        gates = jnp.where(lax.broadcasted_iota(jnp.int32, head.shape, 1) == head, gates_ref[r : r + 1, :], 0.0)
        gates = jnp.sum(gates, axis=1, keepdims=True)
        raw = jnp.sum(gates * jnp.maximum(logits, 0.0), axis=0, keepdims=True)
        scores_ref[r : r + 1, :] = jnp.where(limit_ref[r : r + 1, :] > 0.0, raw, 0.0)
    heads = value_ref.shape[0]
    this = place[0]
    row = 1 - this
    live = live_ref[1:, :] > 0.0
    second = attend_row(live, absorbed[pl.ds(row, 1)][0], rotary[pl.ds(row, 1)][0], cache_ref[...])
    attended = jnp.concatenate([first_ref[...], second], axis=0).astype(jnp.bfloat16)
    head = lax.broadcasted_iota(jnp.int32, (2 * heads, value_ref.shape[2]), 0) % heads
    result = jnp.zeros(head.shape, jnp.float32)
    for n in range(heads):
        product = jnp.dot(attended, value_ref[n], preferred_element_type=jnp.float32)
        result = jnp.where(head == n, product, result)
    for k, row in enumerate((this, 1 - this)):
        out_ref[pl.ds(row, 1)] = result[k * heads : (k + 1) * heads].astype(out_ref.dtype)[None]


def local(
    residual,
    expert_out,
    combine_slot,
    combine_gate,
    attn_gain,
    query_down,
    index_gate,
    latent_gain,
    query_up,
    key_absorb,
    index_query,
    value_up,
    latent_cache,
    index_keys,
    lengths,
    block_list,
):
    n_ctx, n_dp, n_hp = (lax.axis_size(name) for name in ("ctx", "dp", "hp"))
    c, d, h = (lax.axis_index(name) for name in ("ctx", "dp", "hp"))
    rows, features = residual.shape
    qlora = query_down.shape[1]
    selected = block_list.shape[1]
    span, width = latent_cache.shape[1:]
    heads = value_up.shape[0]
    f32, bf16 = jnp.float32, jnp.bfloat16

    slots = expert_out[0]
    received = [lax.ppermute(slots, "dp", shifted(n_dp, step)) for step in range(1, n_dp)]

    index_heads, index_span = index_query.shape[1], index_keys.shape[1]
    sources = [jnp.bitwise_xor(c, step) * n_hp * index_heads for step in range(n_ctx)]
    scalars = [h, c * (span // BLK), c % 2, d, (c * n_hp + h) * index_span, *sources]
    place = in_vmem(jnp.stack(scalars).astype(jnp.int32))
    half = pltpu.VMEM((width, selected // 2 * BLK), bf16)
    mine, send, *ready, live, limit, gain, igate, down = pl.pallas_call(
        functools.partial(prepare, len(received)),
        out_shape=(
            half,
            half,
            pltpu.VMEM((rows, features), f32),
            pltpu.VMEM((len(received), rows, slots.shape[1], LANES), f32),
            pltpu.VMEM((rows, selected * BLK), f32),
            pltpu.VMEM((rows, index_span), f32),
            pltpu.VMEM(attn_gain.shape, f32),
            pltpu.VMEM(index_gate.shape[::-1], bf16),
            pltpu.VMEM(query_down.shape, bf16),
        ),
        in_specs=[SMEM] + [HBM] * 10,
        out_specs=(VMEM,) * 9,
        scratch_shapes=[
            pltpu.SMEM(block_list.shape, jnp.int32),
            pltpu.SMEM(lengths.shape, jnp.int32),
            pltpu.SMEM(combine_slot.shape, jnp.int32),
            pltpu.SMEM(combine_gate.shape, f32),
            pltpu.VMEM((width, span), bf16),
            pltpu.VMEM(slots.shape[1:], bf16),
            pltpu.VMEM(residual.shape, bf16),
            pltpu.SemaphoreType.DMA((4,)),
            pltpu.SemaphoreType.DMA((6,)),
        ],
        compiler_params=limits(6),
        name="prepare",
    )(
        place,
        *map(in_hbm, (block_list, lengths, combine_slot, combine_gate)),
        *map(in_hbm, (jnp.swapaxes(latent_cache, 1, 2), slots, residual, attn_gain, index_gate.T, query_down)),
    )
    upper, lower = (lax.ppermute(x, "ctx", swapped(n_ctx, 1)) for x in (send[: width // 2], send[width // 2 :]))
    ready = [*ready, gain, igate, down]
    received, ready = lax.optimization_barrier((received, ready))

    hidden, part = pl.pallas_call(
        functools.partial(combine_down, len(received)),
        out_shape=(
            jax.ShapeDtypeStruct((rows, features), bf16),
            pltpu.VMEM((rows, qlora + 2 * LANES), f32),
        ),
        in_specs=[SMEM] + [VMEM] * (5 + len(received)),
        out_specs=(VMEM, VMEM),
        compiler_params=limits(8),
        cost_estimate=pl.CostEstimate(flops=10000000000, bytes_accessed=0, transcendentals=0),
        name="combine_down",
    )(place, *map(in_vmem, ready), *received)

    mine, upper, lower, _ = lax.optimization_barrier((mine, upper, lower, part))
    mine = mine + jnp.concatenate([upper, lower], axis=0)
    crossed = [lax.ppermute(mine, "ctx", swapped(n_ctx, 2))]

    parts = [part] + [lax.ppermute(part, "ctx", swapped(n_ctx, step)) for step in range(1, n_ctx)]
    total = functools.reduce(jnp.add, parts)
    scale = lax.rsqrt(total[:, qlora + LANES : qlora + LANES + 1] / D + epsilon)
    latent_sum = total[:, :qlora] * scale
    head_gate = total[:, qlora : qlora + IHEADS] * (scale * IHEADS**-0.5 * IDIM**-0.5)
    latent_scale = lax.rsqrt(jnp.mean(latent_sum * latent_sum, axis=-1, keepdims=True) + epsilon)
    latent = (latent_sum * latent_scale * latent_gain).astype(bf16)

    index_local = jnp.einsum("rq,qnd->nrd", latent, index_query, preferred_element_type=f32).astype(bf16)
    index_other = lax.ppermute(index_local, "hp", swapped(n_hp, 1))
    projected = jnp.einsum("rq,qnd->rnd", latent, query_up, preferred_element_type=f32).astype(bf16)
    absorbed = jnp.einsum("rnk,nkc->rnc", projected[:, :, :NOPE], key_absorb, preferred_element_type=f32).astype(bf16)
    rotary = projected[:, :, NOPE:]
    index_local, index_other, mine, crossed, absorbed, rotary = lax.optimization_barrier(
        (index_local, index_other, mine, crossed, absorbed, rotary)
    )
    index_pair = jnp.stack([index_local, index_other])
    gathered = [index_pair] + [lax.ppermute(index_pair, "ctx", swapped(n_ctx, step)) for step in range(1, n_ctx)]

    mine = functools.reduce(jnp.add, crossed, mine)
    bit = 4
    while bit < n_ctx:
        mine = mine + lax.ppermute(mine, "ctx", swapped(n_ctx, bit))
        bit *= 2
    other = lax.ppermute(mine, "ctx", swapped(n_ctx, 1))
    mine = jnp.concatenate([mine, other], axis=1)
    theirs = lax.ppermute(mine, "hp", swapped(n_hp, 1))
    attended = pl.pallas_call(
        attend_first,
        out_shape=pltpu.VMEM((heads, KVLORA), f32),
        in_specs=[SMEM] + [VMEM] * 4,
        out_specs=VMEM,
        compiler_params=limits(4),
        cost_estimate=pl.CostEstimate(flops=20000000000, bytes_accessed=0, transcendentals=0),
        name="attend_first",
    )(place, *map(in_vmem, (live, absorbed, rotary, mine)))
    gathered, attended = lax.optimization_barrier((gathered, attended))
    attn_out, index_scores = pl.pallas_call(
        functools.partial(finish, n_ctx),
        out_shape=(
            jax.ShapeDtypeStruct((rows, heads, value_up.shape[2]), bf16),
            jax.ShapeDtypeStruct((rows, index_span), f32),
        ),
        in_specs=[SMEM] + [VMEM] * (9 + n_ctx),
        out_specs=(VMEM, VMEM),
        scratch_shapes=[pltpu.VMEM((rows, IHEADS, IDIM), f32)],
        compiler_params=limits(8),
        name="finish",
    )(
        place,
        *map(in_vmem, (live, absorbed, rotary, attended, theirs, value_up, limit, head_gate, index_keys, *gathered)),
    )
    return (hidden, index_scores, attn_out)


def solution(mesh):
    placed = (
        P(("groups", "dp"), "ctx"),
        P(("groups", "dp"), None, None, "ctx"),
        P(("groups", "dp"), None),
        P(("groups", "dp"), None),
        P("ctx"),
        P("ctx", None),
        P("ctx", None),
        P(),
        P(None, ("ctx", "hp"), None),
        P(("ctx", "hp"), None, None),
        P(None, ("ctx", "hp"), None),
        P(("ctx", "hp"), None, None),
        P(("groups", "dp"), "ctx", None),
        P(("groups", "dp"), ("ctx", "hp"), None),
        P(("groups", "dp")),
        P(("groups", "dp"), None),
    )
    return jax.shard_map(
        local,
        mesh=mesh,
        in_specs=placed,
        out_specs=(
            P(("groups", "dp"), "ctx"),
            P(("groups", "dp"), ("ctx", "hp")),
            P(("groups", "dp"), ("ctx", "hp"), None),
        ),
        check_vma=False,
    )
```

```python
import functools

import jax
import jax.numpy as jnp
from jax import lax
from jax.experimental import pallas as pl
from jax.experimental.pallas import tpu as pltpu
from jax.sharding import PartitionSpec as P

D = 7168
KVLORA = 512
ROPE = 64
NOPE = 128
IHEADS = 64
IDIM = 128
BLK = 64
LANES = 128


epsilon = 1e-06
very_low = -1e30

SMEM = pl.BlockSpec(memory_space=pltpu.SMEM)
VMEM = pl.BlockSpec(memory_space=pltpu.VMEM)
HBM = pl.BlockSpec(memory_space=pltpu.HBM)
NT = (((1,), (1,)), ((), ()))


def shifted(size, step):
    return [(i, (i + step) % size) for i in range(size)]


def swapped(size, bit):
    return [(i, i ^ bit) for i in range(size)]


def limits(mib):
    return pltpu.CompilerParams(vmem_limit_bytes=mib << 20)


def in_hbm(array):
    return pltpu.with_memory_space_constraint(array, pltpu.HBM)


def in_vmem(array):
    return pltpu.with_memory_space_constraint(array, pltpu.VMEM)


def prepare(
    sources, place, blocks_hbm, lengths_hbm, slot_hbm, gate_hbm, cache_ref, slots_ref, residual_ref, gain_ref, igate_ref,
    keep_ref, send_ref, base_ref, weight_ref, live_ref, limit_ref, gain_out_ref, igate_out_ref,
    blocks_ref, lengths_ref, slot_ref, gate_ref, cache, own, residual, scalar_sems, sems,
):
    this, group = place[0], place[3]
    width = cache_ref.shape[1]
    count = blocks_hbm.shape[1]
    scalars = ((blocks_hbm, blocks_ref), (lengths_hbm, lengths_ref), (slot_hbm, slot_ref), (gate_hbm, gate_ref))
    fetched = [pltpu.make_async_copy(source, target, scalar_sems.at[k]) for k, (source, target) in enumerate(scalars)]
    for copy in fetched:
        copy.start()
    moved = (
        (cache_ref.at[this], cache), (slots_ref.at[group], own), (residual_ref, residual), (gain_ref, gain_out_ref),
        (igate_ref, igate_out_ref),
    )
    moves = [pltpu.make_async_copy(source, target, sems.at[k]) for k, (source, target) in enumerate(moved)]
    for move in moves:
        move.start()
    for copy in fetched:
        copy.wait()
    spots = []
    for slot in range(count):
        local = blocks_ref[this, lax.rem(slot + place[2] * (count // 2), count)] - place[1]
        owned = (local >= 0) & (local < cache_ref.shape[2] // BLK)
        local = jnp.where(owned, local, 0)
        begin = pl.multiple_of(local // 2 * LANES, LANES)
        spots.append((begin, owned, (local % 2) != (slot % 2)))
    rows = residual.shape[0]
    lane = lax.broadcasted_iota(jnp.int32, (1, live_ref.shape[1]), 1)
    for k, row in enumerate((this, 1 - this)):
        position = lane % BLK
        for slot in range(count):
            block = blocks_ref[row, lax.rem(slot + place[2] * (count // 2), count)]
            position = position + jnp.where(lane // BLK == slot, block * BLK, 0)
        live_ref[k : k + 1, :] = (position < lengths_ref[row]).astype(jnp.float32)
    position = place[4] + lax.broadcasted_iota(jnp.int32, (1, limit_ref.shape[1]), 1)
    for r in range(rows):
        limit_ref[r : r + 1, :] = (position < lengths_ref[r]).astype(jnp.float32)
    capacity = own.shape[0]
    spot = lax.broadcasted_iota(jnp.int32, (capacity, LANES), 0)
    weights = []
    for step in range(sources + 1):
        source = lax.rem(group + sources + 1 - step, sources + 1)
        for r in range(rows):
            weight = jnp.zeros(spot.shape, jnp.float32)
            for k in range(slot_ref.shape[1]):
                weight = jnp.where(spot == slot_ref[r, k] - source * capacity, gate_ref[r, k], weight)
            if step == 0:
                weights.append(weight[:, :1])
            else:
                weight_ref[step - 1, r] = weight
    moves[0].wait()
    lane = lax.broadcasted_iota(jnp.int32, (width, LANES), 1)
    for pair in range(count // 2):
        total = jnp.zeros((width, LANES), jnp.float32)
        for side in range(2):
            begin, owned, swap = spots[2 * pair + side]
            tile = cache[:, pl.ds(begin, LANES)].astype(jnp.float32)
            tile = jnp.where(swap, pltpu.roll(tile, BLK, 1), tile)
            total = jnp.where((lane // BLK == side) & owned, tile, total)
        out_ref = keep_ref if 4 * pair < count else send_ref
        begin = pair % (count // 4) * LANES
        out_ref[:, begin : begin + LANES] = total.astype(out_ref.dtype)
    for move in moves[1:]:
        move.wait()
    for r in range(rows):
        routed = jnp.sum(weights[r] * own[...].astype(jnp.float32), axis=0, keepdims=True)
        base_ref[r : r + 1, :] = residual[r : r + 1].astype(jnp.float32) + routed


def combine(sources, place, base_ref, weight_ref, gain_ref, igate_ref, *refs):
    received = refs[:sources]
    hidden_ref, scaled_ref, side_ref = refs[sources:]
    rows = base_ref.shape[0]
    group = place[3]
    routed = [base_ref[r : r + 1, :] for r in range(rows)]
    for k, ref in enumerate(received):
        piece = ref[pl.ds(group, 1)][0].astype(jnp.float32)
        for r in range(rows):
            routed[r] = routed[r] + jnp.sum(weight_ref[k, r][:, :1] * piece, axis=0, keepdims=True)
    hidden = jnp.concatenate(routed, axis=0).astype(jnp.bfloat16)
    hidden_ref[...] = hidden
    widened = hidden.astype(jnp.float32)
    scaled = (widened * gain_ref[...].reshape(1, -1)).astype(jnp.bfloat16)
    scaled_ref[...] = scaled
    squares = jnp.sum(widened * widened, axis=1, keepdims=True)
    side_ref[:, LANES:] = jnp.broadcast_to(squares, (rows, LANES))
    gates = lax.dot_general(scaled, igate_ref[...], NT, preferred_element_type=jnp.float32)
    side_ref[:, :LANES] = jnp.concatenate([gates, gates], axis=1)


def attend_row(live, content, turn, cache):
    logits = jnp.dot(content, cache[:KVLORA], preferred_element_type=jnp.float32) + jnp.dot(
        turn, cache[KVLORA:], preferred_element_type=jnp.float32
    )
    masked = jnp.where(live, logits * (NOPE + ROPE) ** -0.5, very_low)
    weights = jnp.where(live, jnp.exp(masked - jnp.max(masked, axis=1, keepdims=True)), 0.0)
    total = jnp.sum(weights, axis=1, keepdims=True)
    merged = lax.dot_general(weights.astype(jnp.bfloat16), cache[:KVLORA], NT, preferred_element_type=jnp.float32)
    return merged / total


def attend_first(place, live_ref, absorbed, rotary, cache_ref, out_ref):
    row = place[0]
    live = live_ref[:1, :] > 0.0
    out_ref[...] = attend_row(live, absorbed[pl.ds(row, 1)][0], rotary[pl.ds(row, 1)][0], cache_ref[...])


def finish(
    pieces, place, live_ref, absorbed, rotary, first_ref, cache_ref, value_ref, limit_ref, gates_ref, keys_ref, held_ref, *refs
):
    gathered = refs[:pieces]
    out_ref, scores_ref, hidden_ref, queries = refs[pieces:]
    hidden_ref[...] = held_ref[...]
    index_heads = gathered[0].shape[1]
    order = lax.broadcasted_iota(jnp.int32, (IHEADS, IHEADS), 0)
    head = order
    for k, ref in enumerate(gathered):
        for side in range(2):
            spot = 2 * k + side
            begin = place[5 + k] + jnp.where(place[0] == side, 0, index_heads)
            head = jnp.where(order // index_heads == spot, begin + order % index_heads, head)
            for r in range(scores_ref.shape[0]):
                queries[r, spot * index_heads : (spot + 1) * index_heads, :] = ref[side, :, r, :].astype(jnp.float32)
    for r in range(scores_ref.shape[0]):
        logits = lax.dot_general(
            queries[r].astype(jnp.bfloat16), keys_ref[r], NT, preferred_element_type=jnp.float32
        )
        gates = jnp.where(lax.broadcasted_iota(jnp.int32, head.shape, 1) == head, gates_ref[r : r + 1, :], 0.0)
        gates = jnp.sum(gates, axis=1, keepdims=True)
        raw = jnp.sum(gates * jnp.maximum(logits, 0.0), axis=0, keepdims=True)
        scores_ref[r : r + 1, :] = jnp.where(limit_ref[r : r + 1, :] > 0.0, raw, 0.0)
    heads = value_ref.shape[0]
    this = place[0]
    row = 1 - this
    live = live_ref[1:, :] > 0.0
    second = attend_row(live, absorbed[pl.ds(row, 1)][0], rotary[pl.ds(row, 1)][0], cache_ref[...])
    attended = jnp.concatenate([first_ref[...], second], axis=0).astype(jnp.bfloat16)
    head = lax.broadcasted_iota(jnp.int32, (2 * heads, value_ref.shape[2]), 0) % heads
    result = jnp.zeros(head.shape, jnp.float32)
    for n in range(heads):
        product = jnp.dot(attended, value_ref[n], preferred_element_type=jnp.float32)
        result = jnp.where(head == n, product, result)
    for k, row in enumerate((this, 1 - this)):
        out_ref[pl.ds(row, 1)] = result[k * heads : (k + 1) * heads].astype(out_ref.dtype)[None]


def local(
    residual,
    expert_out,
    combine_slot,
    combine_gate,
    attn_gain,
    query_down,
    index_gate,
    latent_gain,
    query_up,
    key_absorb,
    index_query,
    value_up,
    latent_cache,
    index_keys,
    lengths,
    block_list,
):
    n_ctx, n_dp, n_hp = (lax.axis_size(name) for name in ("ctx", "dp", "hp"))
    c, d, h = (lax.axis_index(name) for name in ("ctx", "dp", "hp"))
    rows, features = residual.shape
    qlora = query_down.shape[1]
    selected = block_list.shape[1]
    span, width = latent_cache.shape[1:]
    heads = value_up.shape[0]
    f32, bf16 = jnp.float32, jnp.bfloat16

    slots = expert_out[0]
    received = [lax.ppermute(slots, "dp", shifted(n_dp, step)) for step in range(1, n_dp)]

    index_heads, index_span = index_query.shape[1], index_keys.shape[1]
    sources = [jnp.bitwise_xor(c, step) * n_hp * index_heads for step in range(n_ctx)]
    scalars = [h, c * (span // BLK), c % 2, d, (c * n_hp + h) * index_span, *sources]
    place = in_vmem(jnp.stack(scalars).astype(jnp.int32))
    half = pltpu.VMEM((width, selected // 2 * BLK), bf16)
    mine, send, *ready, live, limit, gain, igate = pl.pallas_call(
        functools.partial(prepare, len(received)),
        out_shape=(
            half,
            half,
            pltpu.VMEM((rows, features), f32),
            pltpu.VMEM((len(received), rows, slots.shape[1], LANES), f32),
            pltpu.VMEM((rows, selected * BLK), f32),
            pltpu.VMEM((rows, index_span), f32),
            pltpu.VMEM(attn_gain.shape, f32),
            pltpu.VMEM(index_gate.shape[::-1], bf16),
        ),
        in_specs=[SMEM] + [HBM] * 9,
        out_specs=(VMEM,) * 8,
        scratch_shapes=[
            pltpu.SMEM(block_list.shape, jnp.int32),
            pltpu.SMEM(lengths.shape, jnp.int32),
            pltpu.SMEM(combine_slot.shape, jnp.int32),
            pltpu.SMEM(combine_gate.shape, f32),
            pltpu.VMEM((width, span), bf16),
            pltpu.VMEM(slots.shape[1:], bf16),
            pltpu.VMEM(residual.shape, bf16),
            pltpu.SemaphoreType.DMA((4,)),
            pltpu.SemaphoreType.DMA((5,)),
        ],
        compiler_params=limits(6),
        cost_estimate=pl.CostEstimate(flops=10000000000, bytes_accessed=0, transcendentals=0),
        name="prepare",
    )(
        place,
        *map(in_hbm, (block_list, lengths, combine_slot, combine_gate)),
        *map(in_hbm, (jnp.swapaxes(latent_cache, 1, 2), slots, residual, attn_gain, index_gate.T)),
    )
    upper, lower = (lax.ppermute(x, "ctx", swapped(n_ctx, 1)) for x in (send[: width // 2], send[width // 2 :]))
    ready = [*ready, gain, igate]
    received, ready = lax.optimization_barrier((received, ready))

    hidden, scaled, side = pl.pallas_call(
        functools.partial(combine, len(received)),
        out_shape=(
            pltpu.VMEM((rows, features), bf16),
            pltpu.VMEM((rows, features), bf16),
            pltpu.VMEM((rows, 2 * LANES), f32),
        ),
        in_specs=[SMEM] + [VMEM] * (4 + len(received)),
        out_specs=(VMEM, VMEM, VMEM),
        compiler_params=limits(4),
        cost_estimate=pl.CostEstimate(flops=10000000000, bytes_accessed=0, transcendentals=0),
        name="combine",
    )(place, *map(in_vmem, ready), *received)
    part = jnp.concatenate([jnp.dot(scaled, query_down, preferred_element_type=f32), side], axis=1)

    mine, upper, lower, _ = lax.optimization_barrier((mine, upper, lower, part))
    mine = mine + jnp.concatenate([upper, lower], axis=0)
    crossed = [lax.ppermute(mine, "ctx", swapped(n_ctx, 2))]

    parts = [part] + [lax.ppermute(part, "ctx", swapped(n_ctx, step)) for step in range(n_ctx - 1, 0, -1)]
    total = functools.reduce(jnp.add, parts)
    scale = lax.rsqrt(total[:, qlora + LANES : qlora + LANES + 1] / D + epsilon)
    latent_sum = total[:, :qlora] * scale
    head_gate = total[:, qlora : qlora + IHEADS] * (scale * IHEADS**-0.5 * IDIM**-0.5)
    latent_scale = lax.rsqrt(jnp.mean(latent_sum * latent_sum, axis=-1, keepdims=True) + epsilon)
    latent = (latent_sum * latent_scale * latent_gain).astype(bf16)

    index_local = jnp.einsum("rq,qnd->nrd", latent, index_query, preferred_element_type=f32).astype(bf16)
    index_other = lax.ppermute(index_local, "hp", swapped(n_hp, 1))
    index_local, latent = lax.optimization_barrier((index_local, latent))
    projected = jnp.einsum("rq,qnd->rnd", latent, query_up, preferred_element_type=f32).astype(bf16)
    absorbed = jnp.einsum("rnk,nkc->rnc", projected[:, :, :NOPE], key_absorb, preferred_element_type=f32).astype(bf16)
    rotary = projected[:, :, NOPE:]
    index_local, index_other, mine, crossed, absorbed, rotary = lax.optimization_barrier(
        (index_local, index_other, mine, crossed, absorbed, rotary)
    )
    index_pair = jnp.stack([index_local, index_other])
    gathered = [index_pair] + [lax.ppermute(index_pair, "ctx", swapped(n_ctx, step)) for step in range(1, n_ctx)]

    mine = functools.reduce(jnp.add, crossed, mine)
    bit = 4
    while bit < n_ctx:
        mine = mine + lax.ppermute(mine, "ctx", swapped(n_ctx, bit))
        bit *= 2
    other = lax.ppermute(mine, "ctx", swapped(n_ctx, 1))
    mine = jnp.concatenate([mine, other], axis=1)
    theirs = lax.ppermute(mine, "hp", swapped(n_hp, 1))
    attended = pl.pallas_call(
        attend_first,
        out_shape=pltpu.VMEM((heads, KVLORA), f32),
        in_specs=[SMEM] + [VMEM] * 4,
        out_specs=VMEM,
        compiler_params=limits(4),
        cost_estimate=pl.CostEstimate(flops=20000000000, bytes_accessed=0, transcendentals=0),
        name="attend_first",
    )(place, *map(in_vmem, (live, absorbed, rotary, mine)))
    gathered, attended = lax.optimization_barrier((gathered, attended))
    attn_out, index_scores, hidden = pl.pallas_call(
        functools.partial(finish, n_ctx),
        out_shape=(
            jax.ShapeDtypeStruct((rows, heads, value_up.shape[2]), bf16),
            jax.ShapeDtypeStruct((rows, index_span), f32),
            jax.ShapeDtypeStruct((rows, features), bf16),
        ),
        in_specs=[SMEM] + [VMEM] * (10 + n_ctx),
        out_specs=(VMEM, VMEM, VMEM),
        scratch_shapes=[pltpu.VMEM((rows, IHEADS, IDIM), f32)],
        compiler_params=limits(8),
        name="finish",
    )(
        place,
        *map(in_vmem, (live, absorbed, rotary, attended, theirs, value_up, limit, head_gate, index_keys, hidden, *gathered)),
    )
    return (hidden, index_scores, attn_out)


def solution(mesh):
    placed = (
        P(("groups", "dp"), "ctx"),
        P(("groups", "dp"), None, None, "ctx"),
        P(("groups", "dp"), None),
        P(("groups", "dp"), None),
        P("ctx"),
        P("ctx", None),
        P("ctx", None),
        P(),
        P(None, ("ctx", "hp"), None),
        P(("ctx", "hp"), None, None),
        P(None, ("ctx", "hp"), None),
        P(("ctx", "hp"), None, None),
        P(("groups", "dp"), "ctx", None),
        P(("groups", "dp"), ("ctx", "hp"), None),
        P(("groups", "dp")),
        P(("groups", "dp"), None),
    )
    return jax.shard_map(
        local,
        mesh=mesh,
        in_specs=placed,
        out_specs=(
            P(("groups", "dp"), "ctx"),
            P(("groups", "dp"), ("ctx", "hp")),
            P(("groups", "dp"), ("ctx", "hp"), None),
        ),
        check_vma=False,
    )
```

```python
import functools

import jax
import jax.numpy as jnp
from jax import lax
from jax.experimental import pallas as pl
from jax.experimental.pallas import tpu as pltpu
from jax.sharding import PartitionSpec as P

D = 7168
KVLORA = 512
ROPE = 64
NOPE = 128
IHEADS = 64
IDIM = 128
BLK = 64
LANES = 128


epsilon = 1e-06
very_low = -1e30

SMEM = pl.BlockSpec(memory_space=pltpu.SMEM)
VMEM = pl.BlockSpec(memory_space=pltpu.VMEM)
HBM = pl.BlockSpec(memory_space=pltpu.HBM)
NT = (((1,), (1,)), ((), ()))


def shifted(size, step):
    return [(i, (i + step) % size) for i in range(size)]


def swapped(size, bit):
    return [(i, i ^ bit) for i in range(size)]


def limits(mib):
    return pltpu.CompilerParams(vmem_limit_bytes=mib << 20)


def in_hbm(array):
    return pltpu.with_memory_space_constraint(array, pltpu.HBM)


def in_vmem(array):
    return pltpu.with_memory_space_constraint(array, pltpu.VMEM)


def prepare(
    sources, place, blocks_hbm, lengths_hbm, slot_hbm, gate_hbm, cache_ref, slots_ref, residual_ref, gain_ref, igate_ref,
    keep_ref, send_ref, base_ref, weight_ref, live_ref, limit_ref, gain_out_ref, igate_out_ref,
    blocks_ref, lengths_ref, slot_ref, gate_ref, cache, own, residual, scalar_sems, sems,
):
    this, group = place[0], place[3]
    width = cache_ref.shape[1]
    count = blocks_hbm.shape[1]
    scalars = ((blocks_hbm, blocks_ref), (lengths_hbm, lengths_ref), (slot_hbm, slot_ref), (gate_hbm, gate_ref))
    fetched = [pltpu.make_async_copy(source, target, scalar_sems.at[k]) for k, (source, target) in enumerate(scalars)]
    for copy in fetched:
        copy.start()
    moved = (
        (cache_ref.at[this], cache), (slots_ref.at[group], own), (residual_ref, residual), (gain_ref, gain_out_ref),
        (igate_ref, igate_out_ref),
    )
    moves = [pltpu.make_async_copy(source, target, sems.at[k]) for k, (source, target) in enumerate(moved)]
    for move in moves:
        move.start()
    for copy in fetched:
        copy.wait()
    spots = []
    for slot in range(count):
        local = blocks_ref[this, lax.rem(slot + place[2] * (count // 2), count)] - place[1]
        owned = (local >= 0) & (local < cache_ref.shape[2] // BLK)
        local = jnp.where(owned, local, 0)
        begin = pl.multiple_of(local // 2 * LANES, LANES)
        spots.append((begin, owned, (local % 2) != (slot % 2)))
    rows = residual.shape[0]
    lane = lax.broadcasted_iota(jnp.int32, (1, live_ref.shape[1]), 1)
    for k, row in enumerate((this, 1 - this)):
        position = lane % BLK
        for slot in range(count):
            block = blocks_ref[row, lax.rem(slot + place[2] * (count // 2), count)]
            position = position + jnp.where(lane // BLK == slot, block * BLK, 0)
        live_ref[k : k + 1, :] = (position < lengths_ref[row]).astype(jnp.float32)
    position = place[4] + lax.broadcasted_iota(jnp.int32, (1, limit_ref.shape[1]), 1)
    for r in range(rows):
        limit_ref[r : r + 1, :] = (position < lengths_ref[r]).astype(jnp.float32)
    capacity = own.shape[0]
    spot = lax.broadcasted_iota(jnp.int32, (capacity, LANES), 0)
    weights = []
    for step in range(sources + 1):
        source = lax.rem(group + sources + 1 - step, sources + 1)
        for r in range(rows):
            weight = jnp.zeros(spot.shape, jnp.float32)
            for k in range(slot_ref.shape[1]):
                weight = jnp.where(spot == slot_ref[r, k] - source * capacity, gate_ref[r, k], weight)
            if step == 0:
                weights.append(weight[:, :1])
            else:
                weight_ref[step - 1, r] = weight
    moves[0].wait()
    lane = lax.broadcasted_iota(jnp.int32, (width, LANES), 1)
    for pair in range(count // 2):
        total = jnp.zeros((width, LANES), jnp.float32)
        for side in range(2):
            begin, owned, swap = spots[2 * pair + side]
            tile = cache[:, pl.ds(begin, LANES)].astype(jnp.float32)
            tile = jnp.where(swap, pltpu.roll(tile, BLK, 1), tile)
            total = jnp.where((lane // BLK == side) & owned, tile, total)
        out_ref = keep_ref if 4 * pair < count else send_ref
        begin = pair % (count // 4) * LANES
        out_ref[:, begin : begin + LANES] = total.astype(out_ref.dtype)
    for move in moves[1:]:
        move.wait()
    for r in range(rows):
        routed = jnp.sum(weights[r] * own[...].astype(jnp.float32), axis=0, keepdims=True)
        base_ref[r : r + 1, :] = residual[r : r + 1].astype(jnp.float32) + routed


def combine(sources, place, base_ref, weight_ref, gain_ref, igate_ref, *refs):
    received = refs[:sources]
    hidden_ref, scaled_ref, side_ref = refs[sources:]
    rows = base_ref.shape[0]
    group = place[3]
    routed = [base_ref[r : r + 1, :] for r in range(rows)]
    for k, ref in enumerate(received):
        piece = ref[pl.ds(group, 1)][0].astype(jnp.float32)
        for r in range(rows):
            routed[r] = routed[r] + jnp.sum(weight_ref[k, r][:, :1] * piece, axis=0, keepdims=True)
    hidden = jnp.concatenate(routed, axis=0).astype(jnp.bfloat16)
    hidden_ref[...] = hidden
    widened = hidden.astype(jnp.float32)
    scaled = (widened * gain_ref[...].reshape(1, -1)).astype(jnp.bfloat16)
    scaled_ref[...] = scaled
    squares = jnp.sum(widened * widened, axis=1, keepdims=True)
    side_ref[:, LANES:] = jnp.broadcast_to(squares, (rows, LANES))
    gates = lax.dot_general(scaled, igate_ref[...], NT, preferred_element_type=jnp.float32)
    side_ref[:, :LANES] = jnp.concatenate([gates, gates], axis=1)


def attend_row(live, content, turn, cache):
    logits = jnp.dot(content, cache[:KVLORA], preferred_element_type=jnp.float32) + jnp.dot(
        turn, cache[KVLORA:], preferred_element_type=jnp.float32
    )
    masked = jnp.where(live, logits * (NOPE + ROPE) ** -0.5, very_low)
    weights = jnp.where(live, jnp.exp(masked - jnp.max(masked, axis=1, keepdims=True)), 0.0)
    total = jnp.sum(weights, axis=1, keepdims=True)
    merged = lax.dot_general(weights.astype(jnp.bfloat16), cache[:KVLORA], NT, preferred_element_type=jnp.float32)
    return merged / total


def attend_first(place, live_ref, absorbed, rotary, cache_ref, out_ref):
    row = place[0]
    live = live_ref[:1, :] > 0.0
    out_ref[...] = attend_row(live, absorbed[pl.ds(row, 1)][0], rotary[pl.ds(row, 1)][0], cache_ref[...])


def finish(
    pieces, place, live_ref, absorbed, rotary, first_ref, cache_ref, value_ref, limit_ref, gates_ref, keys_ref, held_ref, *refs
):
    gathered = refs[:pieces]
    out_ref, scores_ref, hidden_ref, queries = refs[pieces:]
    hidden_ref[...] = held_ref[...]
    index_heads = gathered[0].shape[1]
    order = lax.broadcasted_iota(jnp.int32, (IHEADS, IHEADS), 0)
    head = order
    for k, ref in enumerate(gathered):
        for side in range(2):
            spot = 2 * k + side
            begin = place[5 + k] + jnp.where(place[0] == side, 0, index_heads)
            head = jnp.where(order // index_heads == spot, begin + order % index_heads, head)
            for r in range(scores_ref.shape[0]):
                queries[r, spot * index_heads : (spot + 1) * index_heads, :] = ref[side, :, r, :].astype(jnp.float32)
    for r in range(scores_ref.shape[0]):
        logits = lax.dot_general(
            queries[r].astype(jnp.bfloat16), keys_ref[r], NT, preferred_element_type=jnp.float32
        )
        gates = jnp.where(lax.broadcasted_iota(jnp.int32, head.shape, 1) == head, gates_ref[r : r + 1, :], 0.0)
        gates = jnp.sum(gates, axis=1, keepdims=True)
        raw = jnp.sum(gates * jnp.maximum(logits, 0.0), axis=0, keepdims=True)
        scores_ref[r : r + 1, :] = jnp.where(limit_ref[r : r + 1, :] > 0.0, raw, 0.0)
    heads = value_ref.shape[0]
    this = place[0]
    row = 1 - this
    live = live_ref[1:, :] > 0.0
    second = attend_row(live, absorbed[pl.ds(row, 1)][0], rotary[pl.ds(row, 1)][0], cache_ref[...])
    attended = jnp.concatenate([first_ref[...], second], axis=0).astype(jnp.bfloat16)
    head = lax.broadcasted_iota(jnp.int32, (2 * heads, value_ref.shape[2]), 0) % heads
    result = jnp.zeros(head.shape, jnp.float32)
    for n in range(heads):
        product = jnp.dot(attended, value_ref[n], preferred_element_type=jnp.float32)
        result = jnp.where(head == n, product, result)
    for k, row in enumerate((this, 1 - this)):
        out_ref[pl.ds(row, 1)] = result[k * heads : (k + 1) * heads].astype(out_ref.dtype)[None]


def local(
    residual,
    expert_out,
    combine_slot,
    combine_gate,
    attn_gain,
    query_down,
    index_gate,
    latent_gain,
    query_up,
    key_absorb,
    index_query,
    value_up,
    latent_cache,
    index_keys,
    lengths,
    block_list,
):
    n_ctx, n_dp, n_hp = (lax.axis_size(name) for name in ("ctx", "dp", "hp"))
    c, d, h = (lax.axis_index(name) for name in ("ctx", "dp", "hp"))
    rows, features = residual.shape
    qlora = query_down.shape[1]
    selected = block_list.shape[1]
    span, width = latent_cache.shape[1:]
    heads = value_up.shape[0]
    f32, bf16 = jnp.float32, jnp.bfloat16

    slots = expert_out[0]
    received = [lax.ppermute(slots, "dp", shifted(n_dp, step)) for step in range(1, n_dp)]

    index_heads, index_span = index_query.shape[1], index_keys.shape[1]
    sources = [jnp.bitwise_xor(c, step) * n_hp * index_heads for step in (0, *range(n_ctx - 1, 0, -1))]
    scalars = [h, c * (span // BLK), c % 2, d, (c * n_hp + h) * index_span, *sources]
    place = in_vmem(jnp.stack(scalars).astype(jnp.int32))
    half = pltpu.VMEM((width, selected // 2 * BLK), bf16)
    mine, send, *ready, live, limit, gain, igate = pl.pallas_call(
        functools.partial(prepare, len(received)),
        out_shape=(
            half,
            half,
            pltpu.VMEM((rows, features), f32),
            pltpu.VMEM((len(received), rows, slots.shape[1], LANES), f32),
            pltpu.VMEM((rows, selected * BLK), f32),
            pltpu.VMEM((rows, index_span), f32),
            pltpu.VMEM(attn_gain.shape, f32),
            pltpu.VMEM(index_gate.shape[::-1], bf16),
        ),
        in_specs=[SMEM] + [HBM] * 9,
        out_specs=(VMEM,) * 8,
        scratch_shapes=[
            pltpu.SMEM(block_list.shape, jnp.int32),
            pltpu.SMEM(lengths.shape, jnp.int32),
            pltpu.SMEM(combine_slot.shape, jnp.int32),
            pltpu.SMEM(combine_gate.shape, f32),
            pltpu.VMEM((width, span), bf16),
            pltpu.VMEM(slots.shape[1:], bf16),
            pltpu.VMEM(residual.shape, bf16),
            pltpu.SemaphoreType.DMA((4,)),
            pltpu.SemaphoreType.DMA((5,)),
        ],
        compiler_params=limits(6),
        cost_estimate=pl.CostEstimate(flops=10000000000, bytes_accessed=0, transcendentals=0),
        name="prepare",
    )(
        place,
        *map(in_hbm, (block_list, lengths, combine_slot, combine_gate)),
        *map(in_hbm, (jnp.swapaxes(latent_cache, 1, 2), slots, residual, attn_gain, index_gate.T)),
    )
    neighbour = lax.ppermute(send, "ctx", swapped(n_ctx, 1))
    ready = [*ready, gain, igate]
    received, ready = lax.optimization_barrier((received, ready))

    hidden, scaled, side = pl.pallas_call(
        functools.partial(combine, len(received)),
        out_shape=(
            pltpu.VMEM((rows, features), bf16),
            pltpu.VMEM((rows, features), bf16),
            pltpu.VMEM((rows, 2 * LANES), f32),
        ),
        in_specs=[SMEM] + [VMEM] * (4 + len(received)),
        out_specs=(VMEM, VMEM, VMEM),
        compiler_params=limits(4),
        cost_estimate=pl.CostEstimate(flops=10000000000, bytes_accessed=0, transcendentals=0),
        name="combine",
    )(place, *map(in_vmem, ready), *received)
    part = jnp.concatenate([jnp.dot(scaled, query_down, preferred_element_type=f32), side], axis=1)

    mine, neighbour, _ = lax.optimization_barrier((mine, neighbour, part))
    mine = mine + neighbour
    mine, near = lax.optimization_barrier((mine, part))
    crossed = [lax.ppermute(mine, "ctx", swapped(n_ctx, 2))]

    parts = [part] + [lax.ppermute(part, "ctx", swapped(n_ctx, step)) for step in range(n_ctx - 1, 1, -1)]
    parts.append(lax.ppermute(near, "ctx", swapped(n_ctx, 1)))
    total = functools.reduce(jnp.add, parts)
    scale = lax.rsqrt(total[:, qlora + LANES : qlora + LANES + 1] / D + epsilon)
    latent_sum = total[:, :qlora] * scale
    head_gate = total[:, qlora : qlora + IHEADS] * (scale * IHEADS**-0.5 * IDIM**-0.5)
    latent_scale = lax.rsqrt(jnp.mean(latent_sum * latent_sum, axis=-1, keepdims=True) + epsilon)
    latent = (latent_sum * latent_scale * latent_gain).astype(bf16)

    index_local = jnp.einsum("rq,qnd->nrd", latent, index_query, preferred_element_type=f32).astype(bf16)
    index_other = lax.ppermute(index_local, "hp", swapped(n_hp, 1))
    index_local, latent = lax.optimization_barrier((index_local, latent))
    projected = jnp.einsum("rq,qnd->rnd", latent, query_up, preferred_element_type=f32).astype(bf16)
    absorbed = jnp.einsum("rnk,nkc->rnc", projected[:, :, :NOPE], key_absorb, preferred_element_type=f32).astype(bf16)
    rotary = projected[:, :, NOPE:]
    index_local, index_other, mine, crossed, absorbed, rotary = lax.optimization_barrier(
        (index_local, index_other, mine, crossed, absorbed, rotary)
    )
    index_pair = jnp.stack([index_local, index_other])
    gathered = [index_pair] + [lax.ppermute(index_pair, "ctx", swapped(n_ctx, step)) for step in range(n_ctx - 1, 0, -1)]

    mine = functools.reduce(jnp.add, crossed, mine)
    bit = 4
    while bit < n_ctx:
        mine = mine + lax.ppermute(mine, "ctx", swapped(n_ctx, bit))
        bit *= 2
    other = lax.ppermute(mine, "ctx", swapped(n_ctx, 1))
    mine = jnp.concatenate([mine, other], axis=1)
    theirs = lax.ppermute(mine, "hp", swapped(n_hp, 1))
    attended = pl.pallas_call(
        attend_first,
        out_shape=pltpu.VMEM((heads, KVLORA), f32),
        in_specs=[SMEM] + [VMEM] * 4,
        out_specs=VMEM,
        compiler_params=limits(4),
        cost_estimate=pl.CostEstimate(flops=20000000000, bytes_accessed=0, transcendentals=0),
        name="attend_first",
    )(place, *map(in_vmem, (live, absorbed, rotary, mine)))
    gathered, attended = lax.optimization_barrier((gathered, attended))
    attn_out, index_scores, hidden = pl.pallas_call(
        functools.partial(finish, n_ctx),
        out_shape=(
            jax.ShapeDtypeStruct((rows, heads, value_up.shape[2]), bf16),
            jax.ShapeDtypeStruct((rows, index_span), f32),
            jax.ShapeDtypeStruct((rows, features), bf16),
        ),
        in_specs=[SMEM] + [VMEM] * (10 + n_ctx),
        out_specs=(VMEM, VMEM, VMEM),
        scratch_shapes=[pltpu.VMEM((rows, IHEADS, IDIM), f32)],
        compiler_params=limits(8),
        name="finish",
    )(
        place,
        *map(in_vmem, (live, absorbed, rotary, attended, theirs, value_up, limit, head_gate, index_keys, hidden, *gathered)),
    )
    return (hidden, index_scores, attn_out)


def solution(mesh):
    placed = (
        P(("groups", "dp"), "ctx"),
        P(("groups", "dp"), None, None, "ctx"),
        P(("groups", "dp"), None),
        P(("groups", "dp"), None),
        P("ctx"),
        P("ctx", None),
        P("ctx", None),
        P(),
        P(None, ("ctx", "hp"), None),
        P(("ctx", "hp"), None, None),
        P(None, ("ctx", "hp"), None),
        P(("ctx", "hp"), None, None),
        P(("groups", "dp"), "ctx", None),
        P(("groups", "dp"), ("ctx", "hp"), None),
        P(("groups", "dp")),
        P(("groups", "dp"), None),
    )
    return jax.shard_map(
        local,
        mesh=mesh,
        in_specs=placed,
        out_specs=(
            P(("groups", "dp"), "ctx"),
            P(("groups", "dp"), ("ctx", "hp")),
            P(("groups", "dp"), ("ctx", "hp"), None),
        ),
        check_vma=False,
    )
```

```python
import functools

import jax
import jax.numpy as jnp
from jax import lax
from jax.experimental import pallas as pl
from jax.experimental.pallas import tpu as pltpu
from jax.sharding import PartitionSpec as P

D = 7168
KVLORA = 512
ROPE = 64
NOPE = 128
IHEADS = 64
IDIM = 128
BLK = 64
LANES = 128


epsilon = 1e-06
very_low = -1e30

SMEM = pl.BlockSpec(memory_space=pltpu.SMEM)
VMEM = pl.BlockSpec(memory_space=pltpu.VMEM)
HBM = pl.BlockSpec(memory_space=pltpu.HBM)
NT = (((1,), (1,)), ((), ()))


def shifted(size, step):
    return [(i, (i + step) % size) for i in range(size)]


def swapped(size, bit):
    return [(i, i ^ bit) for i in range(size)]


def limits(mib):
    return pltpu.CompilerParams(vmem_limit_bytes=mib << 20)


def in_hbm(array):
    return pltpu.with_memory_space_constraint(array, pltpu.HBM)


def in_vmem(array):
    return pltpu.with_memory_space_constraint(array, pltpu.VMEM)


def prepare(
    sources, place, blocks_hbm, lengths_hbm, slot_hbm, gate_hbm, cache_ref, slots_ref, residual_ref, gain_ref, igate_ref,
    keep_ref, send_ref, base_ref, weight_ref, live_ref, limit_ref, gain_out_ref, igate_out_ref,
    blocks_ref, lengths_ref, slot_ref, gate_ref, cache, own, residual, scalar_sems, sems,
):
    this, group = place[0], place[3]
    width = cache_ref.shape[1]
    count = blocks_hbm.shape[1]
    scalars = ((blocks_hbm, blocks_ref), (lengths_hbm, lengths_ref), (slot_hbm, slot_ref), (gate_hbm, gate_ref))
    fetched = [pltpu.make_async_copy(source, target, scalar_sems.at[k]) for k, (source, target) in enumerate(scalars)]
    for copy in fetched:
        copy.start()
    moved = (
        (cache_ref.at[this], cache), (slots_ref.at[group], own), (residual_ref, residual), (gain_ref, gain_out_ref),
        (igate_ref, igate_out_ref),
    )
    moves = [pltpu.make_async_copy(source, target, sems.at[k]) for k, (source, target) in enumerate(moved)]
    for move in moves:
        move.start()
    for copy in fetched:
        copy.wait()
    spots = []
    for slot in range(count):
        local = blocks_ref[this, lax.rem(slot + place[2] * (count // 2), count)] - place[1]
        owned = (local >= 0) & (local < cache_ref.shape[2] // BLK)
        local = jnp.where(owned, local, 0)
        begin = pl.multiple_of(local // 2 * LANES, LANES)
        spots.append((begin, owned, (local % 2) != (slot % 2)))
    rows = residual.shape[0]
    lane = lax.broadcasted_iota(jnp.int32, (1, live_ref.shape[1]), 1)
    for k, row in enumerate((this, 1 - this)):
        position = lane % BLK
        for slot in range(count):
            block = blocks_ref[row, lax.rem(slot + place[2] * (count // 2), count)]
            position = position + jnp.where(lane // BLK == slot, block * BLK, 0)
        live_ref[k : k + 1, :] = (position < lengths_ref[row]).astype(jnp.float32)
    position = place[4] + lax.broadcasted_iota(jnp.int32, (1, limit_ref.shape[1]), 1)
    for r in range(rows):
        limit_ref[r : r + 1, :] = (position < lengths_ref[r]).astype(jnp.float32)
    capacity = own.shape[0]
    spot = lax.broadcasted_iota(jnp.int32, (capacity, LANES), 0)
    weights = []
    for step in range(sources + 1):
        source = lax.rem(group + sources + 1 - step, sources + 1)
        for r in range(rows):
            weight = jnp.zeros(spot.shape, jnp.float32)
            for k in range(slot_ref.shape[1]):
                weight = jnp.where(spot == slot_ref[r, k] - source * capacity, gate_ref[r, k], weight)
            if step == 0:
                weights.append(weight[:, :1])
            else:
                weight_ref[step - 1, r] = weight
    moves[0].wait()
    lane = lax.broadcasted_iota(jnp.int32, (width, LANES), 1)
    for pair in range(count // 2):
        total = jnp.zeros((width, LANES), jnp.float32)
        for side in range(2):
            begin, owned, swap = spots[2 * pair + side]
            tile = cache[:, pl.ds(begin, LANES)].astype(jnp.float32)
            tile = jnp.where(swap, pltpu.roll(tile, BLK, 1), tile)
            total = jnp.where((lane // BLK == side) & owned, tile, total)
        out_ref = keep_ref if 4 * pair < count else send_ref
        begin = pair % (count // 4) * LANES
        out_ref[:, begin : begin + LANES] = total.astype(out_ref.dtype)
    for move in moves[1:]:
        move.wait()
    for r in range(rows):
        routed = jnp.sum(weights[r] * own[...].astype(jnp.float32), axis=0, keepdims=True)
        base_ref[r : r + 1, :] = residual[r : r + 1].astype(jnp.float32) + routed


def combine(sources, place, base_ref, weight_ref, gain_ref, igate_ref, *refs):
    received = refs[:sources]
    hidden_ref, scaled_ref, side_ref = refs[sources:]
    rows = base_ref.shape[0]
    group = place[3]
    routed = [base_ref[r : r + 1, :] for r in range(rows)]
    for k, ref in enumerate(received):
        piece = ref[pl.ds(group, 1)][0].astype(jnp.float32)
        for r in range(rows):
            routed[r] = routed[r] + jnp.sum(weight_ref[k, r][:, :1] * piece, axis=0, keepdims=True)
    hidden = jnp.concatenate(routed, axis=0).astype(jnp.bfloat16)
    hidden_ref[...] = hidden
    widened = hidden.astype(jnp.float32)
    scaled = (widened * gain_ref[...].reshape(1, -1)).astype(jnp.bfloat16)
    scaled_ref[...] = scaled
    squares = jnp.sum(widened * widened, axis=1, keepdims=True)
    side_ref[:, LANES:] = jnp.broadcast_to(squares, (rows, LANES))
    gates = lax.dot_general(scaled, igate_ref[...], NT, preferred_element_type=jnp.float32)
    side_ref[:, :LANES] = jnp.concatenate([gates, gates], axis=1)


def attend_row(live, content, turn, cache):
    logits = jnp.dot(content, cache[:KVLORA], preferred_element_type=jnp.float32) + jnp.dot(
        turn, cache[KVLORA:], preferred_element_type=jnp.float32
    )
    masked = jnp.where(live, logits * (NOPE + ROPE) ** -0.5, very_low)
    weights = jnp.where(live, jnp.exp(masked - jnp.max(masked, axis=1, keepdims=True)), 0.0)
    total = jnp.sum(weights, axis=1, keepdims=True)
    merged = lax.dot_general(weights.astype(jnp.bfloat16), cache[:KVLORA], NT, preferred_element_type=jnp.float32)
    return merged / total


def attend_first(place, live_ref, absorbed, rotary, cache_ref, out_ref):
    row = place[0]
    live = live_ref[:1, :] > 0.0
    out_ref[...] = attend_row(live, absorbed[pl.ds(row, 1)][0], rotary[pl.ds(row, 1)][0], cache_ref[...])


def finish(
    pieces, place, live_ref, absorbed, rotary, first_ref, cache_ref, value_ref, limit_ref, gates_ref, keys_ref, held_ref, *refs
):
    gathered = refs[:pieces]
    out_ref, scores_ref, hidden_ref, queries = refs[pieces:]
    hidden_ref[...] = held_ref[...]
    index_heads = gathered[0].shape[1]
    order = lax.broadcasted_iota(jnp.int32, (IHEADS, IHEADS), 0)
    head = order
    for k, ref in enumerate(gathered):
        for side in range(2):
            spot = 2 * k + side
            begin = place[5 + k] + jnp.where(place[0] == side, 0, index_heads)
            head = jnp.where(order // index_heads == spot, begin + order % index_heads, head)
            for r in range(scores_ref.shape[0]):
                queries[r, spot * index_heads : (spot + 1) * index_heads, :] = ref[side, :, r, :].astype(jnp.float32)
    for r in range(scores_ref.shape[0]):
        logits = lax.dot_general(
            queries[r].astype(jnp.bfloat16), keys_ref[r], NT, preferred_element_type=jnp.float32
        )
        gates = jnp.where(lax.broadcasted_iota(jnp.int32, head.shape, 1) == head, gates_ref[r : r + 1, :], 0.0)
        gates = jnp.sum(gates, axis=1, keepdims=True)
        raw = jnp.sum(gates * jnp.maximum(logits, 0.0), axis=0, keepdims=True)
        scores_ref[r : r + 1, :] = jnp.where(limit_ref[r : r + 1, :] > 0.0, raw, 0.0)
    heads = value_ref.shape[0]
    this = place[0]
    row = 1 - this
    live = live_ref[1:, :] > 0.0
    second = attend_row(live, absorbed[pl.ds(row, 1)][0], rotary[pl.ds(row, 1)][0], cache_ref[...])
    attended = jnp.concatenate([first_ref[...], second], axis=0).astype(jnp.bfloat16)
    head = lax.broadcasted_iota(jnp.int32, (2 * heads, value_ref.shape[2]), 0) % heads
    result = jnp.zeros(head.shape, jnp.float32)
    for n in range(heads):
        product = jnp.dot(attended, value_ref[n], preferred_element_type=jnp.float32)
        result = jnp.where(head == n, product, result)
    for k, row in enumerate((this, 1 - this)):
        out_ref[pl.ds(row, 1)] = result[k * heads : (k + 1) * heads].astype(out_ref.dtype)[None]


def local(
    residual,
    expert_out,
    combine_slot,
    combine_gate,
    attn_gain,
    query_down,
    index_gate,
    latent_gain,
    query_up,
    key_absorb,
    index_query,
    value_up,
    latent_cache,
    index_keys,
    lengths,
    block_list,
):
    n_ctx, n_dp, n_hp = (lax.axis_size(name) for name in ("ctx", "dp", "hp"))
    c, d, h = (lax.axis_index(name) for name in ("ctx", "dp", "hp"))
    rows, features = residual.shape
    qlora = query_down.shape[1]
    selected = block_list.shape[1]
    span, width = latent_cache.shape[1:]
    heads = value_up.shape[0]
    f32, bf16 = jnp.float32, jnp.bfloat16

    slots = expert_out[0]
    received = [lax.ppermute(slots, "dp", shifted(n_dp, step)) for step in range(1, n_dp)]

    index_heads, index_span = index_query.shape[1], index_keys.shape[1]
    sources = [jnp.bitwise_xor(c, step) * n_hp * index_heads for step in (0, *range(n_ctx - 1, 0, -1))]
    scalars = [h, c * (span // BLK), c % 2, d, (c * n_hp + h) * index_span, *sources]
    place = in_vmem(jnp.stack(scalars).astype(jnp.int32))
    half = pltpu.VMEM((width, selected // 2 * BLK), bf16)
    mine, send, *ready, live, limit, gain, igate = pl.pallas_call(
        functools.partial(prepare, len(received)),
        out_shape=(
            half,
            half,
            pltpu.VMEM((rows, features), f32),
            pltpu.VMEM((len(received), rows, slots.shape[1], LANES), f32),
            pltpu.VMEM((rows, selected * BLK), f32),
            pltpu.VMEM((rows, index_span), f32),
            pltpu.VMEM(attn_gain.shape, f32),
            pltpu.VMEM(index_gate.shape[::-1], bf16),
        ),
        in_specs=[SMEM] + [HBM] * 9,
        out_specs=(VMEM,) * 8,
        scratch_shapes=[
            pltpu.SMEM(block_list.shape, jnp.int32),
            pltpu.SMEM(lengths.shape, jnp.int32),
            pltpu.SMEM(combine_slot.shape, jnp.int32),
            pltpu.SMEM(combine_gate.shape, f32),
            pltpu.VMEM((width, span), bf16),
            pltpu.VMEM(slots.shape[1:], bf16),
            pltpu.VMEM(residual.shape, bf16),
            pltpu.SemaphoreType.DMA((4,)),
            pltpu.SemaphoreType.DMA((5,)),
        ],
        compiler_params=limits(6),
        cost_estimate=pl.CostEstimate(flops=10000000000, bytes_accessed=0, transcendentals=0),
        name="prepare",
    )(
        place,
        *map(in_hbm, (block_list, lengths, combine_slot, combine_gate)),
        *map(in_hbm, (jnp.swapaxes(latent_cache, 1, 2), slots, residual, attn_gain, index_gate.T)),
    )
    neighbour = lax.ppermute(send, "ctx", swapped(n_ctx, 1))
    ready = [*ready, gain, igate]
    received, ready = lax.optimization_barrier((received, ready))

    hidden, scaled, side = pl.pallas_call(
        functools.partial(combine, len(received)),
        out_shape=(
            pltpu.VMEM((rows, features), bf16),
            pltpu.VMEM((rows, features), bf16),
            pltpu.VMEM((rows, 2 * LANES), f32),
        ),
        in_specs=[SMEM] + [VMEM] * (4 + len(received)),
        out_specs=(VMEM, VMEM, VMEM),
        compiler_params=limits(4),
        cost_estimate=pl.CostEstimate(flops=10000000000, bytes_accessed=0, transcendentals=0),
        name="combine",
    )(place, *map(in_vmem, ready), *received)
    part = jnp.concatenate([jnp.dot(scaled, query_down, preferred_element_type=f32), side], axis=1)

    mine, neighbour, _ = lax.optimization_barrier((mine, neighbour, part))
    mine = mine + neighbour
    mine, near = lax.optimization_barrier((mine, part))
    crossed = [lax.ppermute(mine, "ctx", swapped(n_ctx, 2))]

    parts = [part] + [lax.ppermute(part, "ctx", swapped(n_ctx, step)) for step in range(2, n_ctx)]
    parts.append(lax.ppermute(near, "ctx", swapped(n_ctx, 1)))
    total = functools.reduce(jnp.add, parts)
    scale = lax.rsqrt(total[:, qlora + LANES : qlora + LANES + 1] / D + epsilon)
    latent_sum = total[:, :qlora] * scale
    head_gate = total[:, qlora : qlora + IHEADS] * (scale * IHEADS**-0.5 * IDIM**-0.5)
    latent_scale = lax.rsqrt(jnp.mean(latent_sum * latent_sum, axis=-1, keepdims=True) + epsilon)
    latent = (latent_sum * latent_scale * latent_gain).astype(bf16)

    index_local = jnp.einsum("rq,qnd->nrd", latent, index_query, preferred_element_type=f32).astype(bf16)
    index_other = lax.ppermute(index_local, "hp", swapped(n_hp, 1))
    index_local, latent = lax.optimization_barrier((index_local, latent))
    projected = jnp.einsum("rq,qnd->rnd", latent, query_up, preferred_element_type=f32).astype(bf16)
    absorbed = jnp.einsum("rnk,nkc->rnc", projected[:, :, :NOPE], key_absorb, preferred_element_type=f32).astype(bf16)
    rotary = projected[:, :, NOPE:]
    index_local, index_other, mine, crossed, absorbed, rotary = lax.optimization_barrier(
        (index_local, index_other, mine, crossed, absorbed, rotary)
    )
    index_pair = jnp.stack([index_local, index_other])
    gathered = [index_pair] + [lax.ppermute(index_pair, "ctx", swapped(n_ctx, step)) for step in range(n_ctx - 1, 0, -1)]

    mine = functools.reduce(jnp.add, crossed, mine)
    bit = 4
    while bit < n_ctx:
        mine = mine + lax.ppermute(mine, "ctx", swapped(n_ctx, bit))
        bit *= 2
    other = lax.ppermute(mine, "ctx", swapped(n_ctx, 1))
    mine = jnp.concatenate([mine, other], axis=1)
    theirs = lax.ppermute(mine, "hp", swapped(n_hp, 1))
    attended = pl.pallas_call(
        attend_first,
        out_shape=pltpu.VMEM((heads, KVLORA), f32),
        in_specs=[SMEM] + [VMEM] * 4,
        out_specs=VMEM,
        compiler_params=limits(4),
        cost_estimate=pl.CostEstimate(flops=20000000000, bytes_accessed=0, transcendentals=0),
        name="attend_first",
    )(place, *map(in_vmem, (live, absorbed, rotary, mine)))
    gathered, attended = lax.optimization_barrier((gathered, attended))
    attn_out, index_scores, hidden = pl.pallas_call(
        functools.partial(finish, n_ctx),
        out_shape=(
            jax.ShapeDtypeStruct((rows, heads, value_up.shape[2]), bf16),
            jax.ShapeDtypeStruct((rows, index_span), f32),
            jax.ShapeDtypeStruct((rows, features), bf16),
        ),
        in_specs=[SMEM] + [VMEM] * (10 + n_ctx),
        out_specs=(VMEM, VMEM, VMEM),
        scratch_shapes=[pltpu.VMEM((rows, IHEADS, IDIM), f32)],
        compiler_params=limits(8),
        name="finish",
    )(
        place,
        *map(in_vmem, (live, absorbed, rotary, attended, theirs, value_up, limit, head_gate, index_keys, hidden, *gathered)),
    )
    return (hidden, index_scores, attn_out)


def solution(mesh):
    placed = (
        P(("groups", "dp"), "ctx"),
        P(("groups", "dp"), None, None, "ctx"),
        P(("groups", "dp"), None),
        P(("groups", "dp"), None),
        P("ctx"),
        P("ctx", None),
        P("ctx", None),
        P(),
        P(None, ("ctx", "hp"), None),
        P(("ctx", "hp"), None, None),
        P(None, ("ctx", "hp"), None),
        P(("ctx", "hp"), None, None),
        P(("groups", "dp"), "ctx", None),
        P(("groups", "dp"), ("ctx", "hp"), None),
        P(("groups", "dp")),
        P(("groups", "dp"), None),
    )
    return jax.shard_map(
        local,
        mesh=mesh,
        in_specs=placed,
        out_specs=(
            P(("groups", "dp"), "ctx"),
            P(("groups", "dp"), ("ctx", "hp")),
            P(("groups", "dp"), ("ctx", "hp"), None),
        ),
        check_vma=False,
    )
```

```python
import functools

import jax
import jax.numpy as jnp
from jax import lax
from jax.experimental import pallas as pl
from jax.experimental.pallas import tpu as pltpu
from jax.sharding import PartitionSpec as P

D = 7168
KVLORA = 512
ROPE = 64
NOPE = 128
IHEADS = 64
IDIM = 128
BLK = 64
LANES = 128


epsilon = 1e-06
very_low = -1e30

SMEM = pl.BlockSpec(memory_space=pltpu.SMEM)
VMEM = pl.BlockSpec(memory_space=pltpu.VMEM)
HBM = pl.BlockSpec(memory_space=pltpu.HBM)
NT = (((1,), (1,)), ((), ()))


def shifted(size, step):
    return [(i, (i + step) % size) for i in range(size)]


def swapped(size, bit):
    return [(i, i ^ bit) for i in range(size)]


def limits(mib):
    return pltpu.CompilerParams(vmem_limit_bytes=mib << 20)


def in_hbm(array):
    return pltpu.with_memory_space_constraint(array, pltpu.HBM)


def in_vmem(array):
    return pltpu.with_memory_space_constraint(array, pltpu.VMEM)


def prepare(
    sources, place, blocks_hbm, lengths_hbm, slot_hbm, gate_hbm, cache_ref, slots_ref, residual_ref, gain_ref, igate_ref,
    keep_ref, send_ref, base_ref, weight_ref, live_ref, limit_ref, gain_out_ref, igate_out_ref,
    blocks_ref, lengths_ref, slot_ref, gate_ref, cache, own, residual, scalar_sems, sems,
):
    this, group = place[0], place[3]
    width = cache_ref.shape[1]
    count = blocks_hbm.shape[1]
    scalars = ((blocks_hbm, blocks_ref), (lengths_hbm, lengths_ref), (slot_hbm, slot_ref), (gate_hbm, gate_ref))
    fetched = [pltpu.make_async_copy(source, target, scalar_sems.at[k]) for k, (source, target) in enumerate(scalars)]
    for copy in fetched:
        copy.start()
    moved = (
        (cache_ref.at[this], cache), (slots_ref.at[group], own), (residual_ref, residual), (gain_ref, gain_out_ref),
        (igate_ref, igate_out_ref),
    )
    moves = [pltpu.make_async_copy(source, target, sems.at[k]) for k, (source, target) in enumerate(moved)]
    for move in moves:
        move.start()
    for copy in fetched:
        copy.wait()
    spots = []
    for slot in range(count):
        local = blocks_ref[this, lax.rem(slot + place[2] * (count // 2), count)] - place[1]
        owned = (local >= 0) & (local < cache_ref.shape[2] // BLK)
        local = jnp.where(owned, local, 0)
        begin = pl.multiple_of(local // 2 * LANES, LANES)
        spots.append((begin, owned, (local % 2) != (slot % 2)))
    rows = residual.shape[0]
    lane = lax.broadcasted_iota(jnp.int32, (1, live_ref.shape[1]), 1)
    for k, row in enumerate((this, 1 - this)):
        position = lane % BLK
        for slot in range(count):
            block = blocks_ref[row, lax.rem(slot + place[2] * (count // 2), count)]
            position = position + jnp.where(lane // BLK == slot, block * BLK, 0)
        live_ref[k : k + 1, :] = (position < lengths_ref[row]).astype(jnp.float32)
    position = place[4] + lax.broadcasted_iota(jnp.int32, (1, limit_ref.shape[1]), 1)
    for r in range(rows):
        limit_ref[r : r + 1, :] = (position < lengths_ref[r]).astype(jnp.float32)
    capacity = own.shape[0]
    spot = lax.broadcasted_iota(jnp.int32, (capacity, LANES), 0)
    weights = []
    for step in range(sources + 1):
        source = lax.rem(group + sources + 1 - step, sources + 1)
        for r in range(rows):
            weight = jnp.zeros(spot.shape, jnp.float32)
            for k in range(slot_ref.shape[1]):
                weight = jnp.where(spot == slot_ref[r, k] - source * capacity, gate_ref[r, k], weight)
            if step == 0:
                weights.append(weight[:, :1])
            else:
                weight_ref[step - 1, r] = weight
    moves[0].wait()
    lane = lax.broadcasted_iota(jnp.int32, (width, LANES), 1)
    for pair in range(count // 2):
        total = jnp.zeros((width, LANES), jnp.float32)
        for side in range(2):
            begin, owned, swap = spots[2 * pair + side]
            tile = cache[:, pl.ds(begin, LANES)].astype(jnp.float32)
            tile = jnp.where(swap, pltpu.roll(tile, BLK, 1), tile)
            total = jnp.where((lane // BLK == side) & owned, tile, total)
        out_ref = keep_ref if 4 * pair < count else send_ref
        begin = pair % (count // 4) * LANES
        out_ref[:, begin : begin + LANES] = total.astype(out_ref.dtype)
    for move in moves[1:]:
        move.wait()
    for r in range(rows):
        routed = jnp.sum(weights[r] * own[...].astype(jnp.float32), axis=0, keepdims=True)
        base_ref[r : r + 1, :] = residual[r : r + 1].astype(jnp.float32) + routed


def combine(sources, place, base_ref, weight_ref, gain_ref, igate_ref, *refs):
    received = refs[:sources]
    hidden_ref, scaled_ref, side_ref = refs[sources:]
    rows = base_ref.shape[0]
    group = place[3]
    routed = [base_ref[r : r + 1, :] for r in range(rows)]
    for k, ref in enumerate(received):
        piece = ref[pl.ds(group, 1)][0].astype(jnp.float32)
        for r in range(rows):
            routed[r] = routed[r] + jnp.sum(weight_ref[k, r][:, :1] * piece, axis=0, keepdims=True)
    hidden = jnp.concatenate(routed, axis=0).astype(jnp.bfloat16)
    hidden_ref[...] = hidden
    widened = hidden.astype(jnp.float32)
    scaled = (widened * gain_ref[...].reshape(1, -1)).astype(jnp.bfloat16)
    scaled_ref[...] = scaled
    squares = jnp.sum(widened * widened, axis=1, keepdims=True)
    side_ref[:, LANES:] = jnp.broadcast_to(squares, (rows, LANES))
    gates = lax.dot_general(scaled, igate_ref[...], NT, preferred_element_type=jnp.float32)
    side_ref[:, :LANES] = jnp.concatenate([gates, gates], axis=1)


def attend_row(live, content, turn, cache):
    logits = jnp.dot(content, cache[:KVLORA], preferred_element_type=jnp.float32) + jnp.dot(
        turn, cache[KVLORA:], preferred_element_type=jnp.float32
    )
    masked = jnp.where(live, logits * (NOPE + ROPE) ** -0.5, very_low)
    weights = jnp.where(live, jnp.exp(masked - jnp.max(masked, axis=1, keepdims=True)), 0.0)
    total = jnp.sum(weights, axis=1, keepdims=True)
    merged = lax.dot_general(weights.astype(jnp.bfloat16), cache[:KVLORA], NT, preferred_element_type=jnp.float32)
    return merged / total


def attend_first(place, live_ref, projected_ref, absorb_ref, cache_ref, out_ref, absorbed, rotary):
    heads, rows = projected_ref.shape[:2]
    for n in range(heads):
        projected = projected_ref[n]
        query = jnp.dot(projected[:, :NOPE], absorb_ref[n], preferred_element_type=jnp.float32)
        query = query.astype(jnp.bfloat16).astype(jnp.float32)
        turn = projected[:, NOPE:].astype(jnp.float32)
        for r in range(rows):
            absorbed[r, n : n + 1, :] = query[r : r + 1]
            rotary[r, n : n + 1, :] = turn[r : r + 1]
    row = place[0]
    live = live_ref[:1, :] > 0.0
    content = absorbed[pl.ds(row, 1)][0].astype(jnp.bfloat16)
    turn = rotary[pl.ds(row, 1)][0].astype(jnp.bfloat16)
    out_ref[...] = attend_row(live, content, turn, cache_ref[...])


def finish(
    pieces, place, live_ref, absorbed, rotary, first_ref, cache_ref, value_ref, limit_ref, gates_ref, keys_ref, held_ref, *refs
):
    gathered = refs[:pieces]
    out_ref, scores_ref, hidden_ref, queries = refs[pieces:]
    hidden_ref[...] = held_ref[...]
    index_heads = gathered[0].shape[1]
    order = lax.broadcasted_iota(jnp.int32, (IHEADS, IHEADS), 0)
    head = order
    for k, ref in enumerate(gathered):
        for side in range(2):
            spot = 2 * k + side
            begin = place[5 + k] + jnp.where(place[0] == side, 0, index_heads)
            head = jnp.where(order // index_heads == spot, begin + order % index_heads, head)
            for r in range(scores_ref.shape[0]):
                queries[r, spot * index_heads : (spot + 1) * index_heads, :] = ref[side, :, r, :].astype(jnp.float32)
    for r in range(scores_ref.shape[0]):
        logits = lax.dot_general(
            queries[r].astype(jnp.bfloat16), keys_ref[r], NT, preferred_element_type=jnp.float32
        )
        gates = jnp.where(lax.broadcasted_iota(jnp.int32, head.shape, 1) == head, gates_ref[r : r + 1, :], 0.0)
        gates = jnp.sum(gates, axis=1, keepdims=True)
        raw = jnp.sum(gates * jnp.maximum(logits, 0.0), axis=0, keepdims=True)
        scores_ref[r : r + 1, :] = jnp.where(limit_ref[r : r + 1, :] > 0.0, raw, 0.0)
    heads = value_ref.shape[0]
    this = place[0]
    row = 1 - this
    live = live_ref[1:, :] > 0.0
    content = absorbed[pl.ds(row, 1)][0].astype(jnp.bfloat16)
    turn = rotary[pl.ds(row, 1)][0].astype(jnp.bfloat16)
    second = attend_row(live, content, turn, cache_ref[...])
    attended = jnp.concatenate([first_ref[...], second], axis=0).astype(jnp.bfloat16)
    head = lax.broadcasted_iota(jnp.int32, (2 * heads, value_ref.shape[2]), 0) % heads
    result = jnp.zeros(head.shape, jnp.float32)
    for n in range(heads):
        product = jnp.dot(attended, value_ref[n], preferred_element_type=jnp.float32)
        result = jnp.where(head == n, product, result)
    for k, row in enumerate((this, 1 - this)):
        out_ref[pl.ds(row, 1)] = result[k * heads : (k + 1) * heads].astype(out_ref.dtype)[None]


def local(
    residual,
    expert_out,
    combine_slot,
    combine_gate,
    attn_gain,
    query_down,
    index_gate,
    latent_gain,
    query_up,
    key_absorb,
    index_query,
    value_up,
    latent_cache,
    index_keys,
    lengths,
    block_list,
):
    n_ctx, n_dp, n_hp = (lax.axis_size(name) for name in ("ctx", "dp", "hp"))
    c, d, h = (lax.axis_index(name) for name in ("ctx", "dp", "hp"))
    rows, features = residual.shape
    qlora = query_down.shape[1]
    selected = block_list.shape[1]
    span, width = latent_cache.shape[1:]
    heads = value_up.shape[0]
    f32, bf16 = jnp.float32, jnp.bfloat16

    slots = expert_out[0]
    received = [lax.ppermute(slots, "dp", shifted(n_dp, step)) for step in range(1, n_dp)]

    index_heads, index_span = index_query.shape[1], index_keys.shape[1]
    sources = [jnp.bitwise_xor(c, step) * n_hp * index_heads for step in (0, *range(n_ctx - 1, 0, -1))]
    scalars = [h, c * (span // BLK), c % 2, d, (c * n_hp + h) * index_span, *sources]
    place = in_vmem(jnp.stack(scalars).astype(jnp.int32))
    half = pltpu.VMEM((width, selected // 2 * BLK), bf16)
    mine, send, *ready, live, limit, gain, igate = pl.pallas_call(
        functools.partial(prepare, len(received)),
        out_shape=(
            half,
            half,
            pltpu.VMEM((rows, features), f32),
            pltpu.VMEM((len(received), rows, slots.shape[1], LANES), f32),
            pltpu.VMEM((rows, selected * BLK), f32),
            pltpu.VMEM((rows, index_span), f32),
            pltpu.VMEM(attn_gain.shape, f32),
            pltpu.VMEM(index_gate.shape[::-1], bf16),
        ),
        in_specs=[SMEM] + [HBM] * 9,
        out_specs=(VMEM,) * 8,
        scratch_shapes=[
            pltpu.SMEM(block_list.shape, jnp.int32),
            pltpu.SMEM(lengths.shape, jnp.int32),
            pltpu.SMEM(combine_slot.shape, jnp.int32),
            pltpu.SMEM(combine_gate.shape, f32),
            pltpu.VMEM((width, span), bf16),
            pltpu.VMEM(slots.shape[1:], bf16),
            pltpu.VMEM(residual.shape, bf16),
            pltpu.SemaphoreType.DMA((4,)),
            pltpu.SemaphoreType.DMA((5,)),
        ],
        compiler_params=limits(6),
        cost_estimate=pl.CostEstimate(flops=10000000000, bytes_accessed=0, transcendentals=0),
        name="prepare",
    )(
        place,
        *map(in_hbm, (block_list, lengths, combine_slot, combine_gate)),
        *map(in_hbm, (jnp.swapaxes(latent_cache, 1, 2), slots, residual, attn_gain, index_gate.T)),
    )
    neighbour = lax.ppermute(send, "ctx", swapped(n_ctx, 1))
    ready = [*ready, gain, igate]
    received, ready = lax.optimization_barrier((received, ready))

    hidden, scaled, side = pl.pallas_call(
        functools.partial(combine, len(received)),
        out_shape=(
            pltpu.VMEM((rows, features), bf16),
            pltpu.VMEM((rows, features), bf16),
            pltpu.VMEM((rows, 2 * LANES), f32),
        ),
        in_specs=[SMEM] + [VMEM] * (4 + len(received)),
        out_specs=(VMEM, VMEM, VMEM),
        compiler_params=limits(4),
        cost_estimate=pl.CostEstimate(flops=10000000000, bytes_accessed=0, transcendentals=0),
        name="combine",
    )(place, *map(in_vmem, ready), *received)
    part = jnp.concatenate([jnp.dot(scaled, query_down, preferred_element_type=f32), side], axis=1)

    mine, neighbour, _ = lax.optimization_barrier((mine, neighbour, part))
    mine = mine + neighbour
    mine, near = lax.optimization_barrier((mine, part))
    crossed = [lax.ppermute(mine, "ctx", swapped(n_ctx, 2))]

    parts = [part] + [lax.ppermute(part, "ctx", swapped(n_ctx, step)) for step in range(2, n_ctx)]
    parts.append(lax.ppermute(near, "ctx", swapped(n_ctx, 1)))
    total = functools.reduce(jnp.add, parts)
    scale = lax.rsqrt(total[:, qlora + LANES : qlora + LANES + 1] / D + epsilon)
    latent_sum = total[:, :qlora] * scale
    head_gate = total[:, qlora : qlora + IHEADS] * (scale * IHEADS**-0.5 * IDIM**-0.5)
    latent_scale = lax.rsqrt(jnp.mean(latent_sum * latent_sum, axis=-1, keepdims=True) + epsilon)
    latent = (latent_sum * latent_scale * latent_gain).astype(bf16)

    index_local = jnp.einsum("rq,qnd->nrd", latent, index_query, preferred_element_type=f32).astype(bf16)
    index_other = lax.ppermute(index_local, "hp", swapped(n_hp, 1))
    index_local, latent = lax.optimization_barrier((index_local, latent))
    projected = jnp.einsum("rq,qnd->rnd", latent, query_up, preferred_element_type=f32).astype(bf16)
    index_local, index_other, mine, crossed, projected = lax.optimization_barrier(
        (index_local, index_other, mine, crossed, projected)
    )
    index_pair = jnp.stack([index_local, index_other])
    gathered = [index_pair] + [lax.ppermute(index_pair, "ctx", swapped(n_ctx, step)) for step in range(n_ctx - 1, 0, -1)]

    mine = functools.reduce(jnp.add, crossed, mine)
    bit = 4
    while bit < n_ctx:
        mine = mine + lax.ppermute(mine, "ctx", swapped(n_ctx, bit))
        bit *= 2
    other = lax.ppermute(mine, "ctx", swapped(n_ctx, 1))
    mine = jnp.concatenate([mine, other], axis=1)
    theirs = lax.ppermute(mine, "hp", swapped(n_hp, 1))
    attended, absorbed, rotary = pl.pallas_call(
        attend_first,
        out_shape=(
            pltpu.VMEM((heads, KVLORA), f32),
            pltpu.VMEM((rows, heads, KVLORA), f32),
            pltpu.VMEM((rows, heads, ROPE), f32),
        ),
        in_specs=[SMEM] + [VMEM] * 4,
        out_specs=(VMEM, VMEM, VMEM),
        compiler_params=limits(4),
        cost_estimate=pl.CostEstimate(flops=20000000000, bytes_accessed=0, transcendentals=0),
        name="attend_first",
    )(place, *map(in_vmem, (live, jnp.transpose(projected, (1, 0, 2)), key_absorb, mine)))
    gathered, attended = lax.optimization_barrier((gathered, attended))
    attn_out, index_scores, hidden = pl.pallas_call(
        functools.partial(finish, n_ctx),
        out_shape=(
            jax.ShapeDtypeStruct((rows, heads, value_up.shape[2]), bf16),
            jax.ShapeDtypeStruct((rows, index_span), f32),
            jax.ShapeDtypeStruct((rows, features), bf16),
        ),
        in_specs=[SMEM] + [VMEM] * (10 + n_ctx),
        out_specs=(VMEM, VMEM, VMEM),
        scratch_shapes=[pltpu.VMEM((rows, IHEADS, IDIM), f32)],
        compiler_params=limits(8),
        name="finish",
    )(
        place,
        *map(in_vmem, (live, absorbed, rotary, attended, theirs, value_up, limit, head_gate, index_keys, hidden, *gathered)),
    )
    return (hidden, index_scores, attn_out)


def solution(mesh):
    placed = (
        P(("groups", "dp"), "ctx"),
        P(("groups", "dp"), None, None, "ctx"),
        P(("groups", "dp"), None),
        P(("groups", "dp"), None),
        P("ctx"),
        P("ctx", None),
        P("ctx", None),
        P(),
        P(None, ("ctx", "hp"), None),
        P(("ctx", "hp"), None, None),
        P(None, ("ctx", "hp"), None),
        P(("ctx", "hp"), None, None),
        P(("groups", "dp"), "ctx", None),
        P(("groups", "dp"), ("ctx", "hp"), None),
        P(("groups", "dp")),
        P(("groups", "dp"), None),
    )
    return jax.shard_map(
        local,
        mesh=mesh,
        in_specs=placed,
        out_specs=(
            P(("groups", "dp"), "ctx"),
            P(("groups", "dp"), ("ctx", "hp")),
            P(("groups", "dp"), ("ctx", "hp"), None),
        ),
        check_vma=False,
    )
```
